256 devices in a mesh: frames: 32 (over z, x_lo, core), runs: 8 (over y, x_hi).
Axes of the slice: x: 4 (x_hi: 2, x_lo: 2; x = x_hi * 2 + x_lo), y: 4, z: 8, core: 2. Of those that a mesh axis runs over, the one named last changes fastest.
Arguments:
- inputs: bfloat16 [8, 131072, 256], P('runs', 'frames'), may hold values from -6 to 6
- first_layer_weight: bfloat16 [3, 256, 256], replicated, may hold values from -0.21875 to 0.21875
- first_layer_bias: bfloat16 [256], replicated, may hold values from -3 to 3
- second_layer_weight: bfloat16 [3, 256, 256], replicated, may hold values from -0.21875 to 0.21875
- second_layer_bias: bfloat16 [256], replicated, may hold values from -3 to 3
- upstream: bfloat16 [8, 131072, 256], P('runs', 'frames'), may hold values from -6 to 6
Outputs:
- outputs: bfloat16 [8, 131072, 256], P('runs', 'frames')
- grad_input: bfloat16 [8, 131072, 256], P('runs', 'frames')
- grad_w_first: float32 [3, 256, 256], replicated
- grad_b_first: float32 [256], replicated
- grad_w_second: float32 [3, 256, 256], replicated
- grad_b_second: float32 [256], replicated
The draws below stay inside these ranges and needn't reach their ends.
All inputs are finite; a program needn't handle non-finite values.
Results may differ from the reference program's by a relative error of at most 0.007.
Values may be sent and summed in bfloat16 or wider, within the bound.
A program may use at most 128 MiB of HBM per device.

```python
import math
import jax
import jax.numpy as jnp
from jax import lax

C = 256
FIRST_SPACING = 256
SECOND_SPACING = 512
FRAMES = 131072
RUNS = 8


def steps_of(own_key, dims, cuts, least, high):
    def one(axis_at, blocks):
        heights = jax.random.uniform(jax.random.fold_in(jax.random.fold_in(own_key, 6), axis_at), (blocks,), jnp.float32, least / len(cuts), high / len(cuts))
        return jnp.repeat(jnp.exp(heights), dims[axis_at] // blocks).reshape((-1,) + (1,) * (len(dims) - axis_at - 1))

    gain = one(*cuts[0])
    for cut in cuts[1:]:
        gain = gain * one(*cut)
    return gain


def scatter_about(rng, shape, spread, reach, shards=(), kind=jnp.bfloat16):
    entries = jax.random.normal(rng, shape, jnp.float32) * spread
    if len(shards) > 0:
        entries = steps_of(rng, shape, shards, -0.22, 0.18) * entries
    return jnp.clip(entries, min=-reach, max=reach).astype(kind)


def setup_inputs(seed: int = 0) -> dict:
    streams_of = jax.random.split(jax.random.key(seed), 7)
    return {
        "inputs": scatter_about(streams_of[0], (RUNS, FRAMES, C), 1.0, 6.0, ((0, 8), (1, 32))),
        "first_layer_weight": scatter_about(streams_of[1], (3, C, C), (3 * C) ** -0.5, 0.21875),
        "first_layer_bias": scatter_about(streams_of[2], (C,), 0.5, 3.0),
        "second_layer_weight": scatter_about(streams_of[3], (3, C, C), (3 * C) ** -0.5, 0.21875),
        "second_layer_bias": scatter_about(streams_of[4], (C,), 0.5, 3.0),
        "upstream": scatter_about(streams_of[5], (RUNS, FRAMES, C), 1.0, 6.0, ((0, 8), (1, 32))),
    }


def gelu_slope(pre, grad):
    return jax.vjp(jax.nn.gelu, pre)[1](grad)[0]

def causal_conv_apply(receptive_span, weights, bias, dilation):
    frame_count = receptive_span.shape[0]
    padded = jnp.concatenate([jnp.zeros((2 * dilation, receptive_span.shape[1]), receptive_span.dtype), receptive_span], axis=0)
    total = bias.astype(jnp.float32)[None, :]
    for k in range(3):
        start = 2 * dilation - k * dilation
        total = total + jnp.dot(padded[start:start + frame_count], weights[k], preferred_element_type=jnp.float32)
    return total

def causal_conv_weight_gradient(receptive_span, grad, dilation):
    frame_count = receptive_span.shape[0]
    padded = jnp.concatenate([jnp.zeros((2 * dilation, receptive_span.shape[1]), receptive_span.dtype), receptive_span], axis=0)
    pieces = []
    for k in range(3):
        start = 2 * dilation - k * dilation
        pieces.append(jnp.dot(padded[start:start + frame_count].T, grad, preferred_element_type=jnp.float32))
    return jnp.stack(pieces)

def causal_conv_input_gradient(grad, weights, dilation):
    frame_count = grad.shape[0]
    padded = jnp.concatenate([grad, jnp.zeros((2 * dilation, grad.shape[1]), grad.dtype)], axis=0)
    total = jnp.zeros((frame_count, grad.shape[1]), jnp.float32)
    for k in range(3):
        start = k * dilation
        total = total + jnp.dot(padded[start:start + frame_count], weights[k].T, preferred_element_type=jnp.float32)
    return total

def reference(inputs, first_layer_weight, first_layer_bias, second_layer_weight, second_layer_bias, upstream):

    def one_run(pair):
        receptive_span, cotangent = pair
        first_preactivation = causal_conv_apply(receptive_span, first_layer_weight, first_layer_bias, FIRST_SPACING)
        hidden_state = (receptive_span.astype(jnp.float32) + jax.nn.gelu(first_preactivation)).astype(jnp.bfloat16)
        second_preactivation = causal_conv_apply(hidden_state, second_layer_weight, second_layer_bias, SECOND_SPACING)
        result = (hidden_state.astype(jnp.float32) + jax.nn.gelu(second_preactivation)).astype(jnp.bfloat16)
        output_gradient = cotangent.astype(jnp.float32)
        second_layer_gradient = gelu_slope(second_preactivation, output_gradient).astype(jnp.bfloat16)
        second_weight_delta = causal_conv_weight_gradient(hidden_state, second_layer_gradient, SECOND_SPACING)
        db_second = lax.optimization_barrier(jnp.sum(second_layer_gradient.astype(jnp.float32), axis=0))
        hidden_gradient = output_gradient + causal_conv_input_gradient(second_layer_gradient, second_layer_weight, SECOND_SPACING)
        first_layer_gradient = gelu_slope(first_preactivation, hidden_gradient).astype(jnp.bfloat16)
        first_weight_delta = causal_conv_weight_gradient(receptive_span, first_layer_gradient, FIRST_SPACING)
        db_first = lax.optimization_barrier(jnp.sum(first_layer_gradient.astype(jnp.float32), axis=0))
        input_gradient_rows = (hidden_gradient + causal_conv_input_gradient(first_layer_gradient, first_layer_weight, FIRST_SPACING)).astype(jnp.bfloat16)
        return (result, input_gradient_rows, first_weight_delta, db_first, second_weight_delta, db_second)
    result, input_gradient_rows, first_weight_delta, db_first, second_weight_delta, db_second = lax.map(one_run, (inputs, upstream))
    factor = 1.0 / math.sqrt(RUNS * FRAMES)
    return (result, input_gradient_rows, factor * lax.optimization_barrier(jnp.sum(first_weight_delta, axis=0)), factor * lax.optimization_barrier(jnp.sum(db_first, axis=0)), factor * lax.optimization_barrier(jnp.sum(second_weight_delta, axis=0)), factor * lax.optimization_barrier(jnp.sum(db_second, axis=0)))
```

```python
import functools
import math

import jax
import jax.numpy as jnp
from jax import lax
from jax.experimental import pallas as pl
from jax.experimental.pallas import tpu as pltpu
from jax.sharding import PartitionSpec as P

C = 256
D1 = 256
D2 = 512
H1 = 2 * D1
H2 = 2 * D2
R = 512
F32 = jnp.float32
BF16 = jnp.bfloat16
C0 = math.sqrt(2.0 / math.pi)
C1 = C0 * 0.044715
MESH = pl.DeviceIdType.MESH


def gelu_parts(v):
    v2 = v * v
    t = jnp.tanh(v * (C0 + C1 * v2))
    h = 0.5 * v
    act = h + h * t
    slope = (0.5 + 0.5 * t) + (h * (1.0 - t * t)) * (C0 + (3.0 * C1) * v2)
    return act, slope


def dot(a, b):
    return jnp.dot(a, b, preferred_element_type=F32)


class Place:
    sizes = {"core": 2, "x": 4, "y": 4, "z": 8}

    def __init__(self):
        self.f = lax.axis_index("frames")
        self.r = lax.axis_index("runs")
        self.core = lax.rem(self.f, 2)
        self.xl = lax.rem(self.f // 2, 2)
        self.z = self.f // 4
        self.xh = lax.rem(self.r, 2)
        self.y = self.r // 2
        self.x = self.xh * 2 + self.xl

    def index(self, axis):
        return {"core": self.core, "x": self.x, "y": self.y, "z": self.z}[axis]

    def other(self, axis, d):
        return lax.rem(self.index(axis) + d, self.sizes[axis])

    def peer(self, axis, i):
        if axis == "core":
            return (self.f - self.core + i, self.r)
        if axis == "x":
            return (self.z * 4 + lax.rem(i, 2) * 2 + self.core, self.y * 2 + i // 2)
        if axis == "y":
            return (self.f, i * 2 + self.xh)
        return (i * 4 + self.xl * 2 + self.core, self.r)


class Part:
    def __init__(self, place, order, refs, send, recv):
        self.p = place
        self.a, self.b = order
        self.s0, self.r0, self.s1, self.r1, self.s2, self.r2, self.zb, self.fin = refs
        self.send, self.recv = send, recv
        self.sem = 0
        self.open = []

    def put(self, src, dst, to):
        copy = pltpu.make_async_remote_copy(
            src_ref=src,
            dst_ref=dst,
            send_sem=self.send.at[self.sem],
            recv_sem=self.recv.at[self.sem],
            device_id=to,
            device_id_type=MESH,
        )
        self.sem += 1
        copy.start()
        self.open.append(copy)

    def drain(self):
        for copy in self.open:
            copy.wait()
        self.open = []

    def steps(self):
        return [self.step0, self.step1, self.step2, self.step3, self.step4, self.step5, self.step6, self.drain]

    def step0(self):
        o = self.p.other("core", 1)
        self.put(self.s0.at[o], self.r0, self.p.peer("core", o))

    def step1(self):
        self.drain()
        c = self.p.core
        self.s1[...] = (self.s0[c].astype(F32) + self.r0[...].astype(F32)).astype(BF16)
        for d in range(1, 4):
            o = self.p.other(self.a, d)
            self.put(self.s1.at[o], self.r1.at[d - 1], self.p.peer(self.a, o))

    def step2(self):
        self.drain()
        i = self.p.index(self.a)
        total = self.s1[i].astype(F32)
        for d in range(3):
            total = total + self.r1[d].astype(F32)
        self.s2[...] = total.astype(BF16)
        for d in range(1, 4):
            o = self.p.other(self.b, d)
            self.put(self.s2.at[o // 2, lax.rem(o, 2)], self.r2.at[d - 1], self.p.peer(self.b, o))

    def step3(self):
        self.drain()
        i = self.p.index(self.b)
        total = self.s2[i // 2, lax.rem(i, 2)].astype(F32)
        for d in range(3):
            total = total + self.r2[d].astype(F32)
        z = self.p.z
        self.zb[z] = total.astype(BF16)
        for d in range(1, 8):
            o = self.p.other("z", d)
            self.put(self.zb.at[z], self.zb.at[z], self.p.peer("z", o))

    def step4(self):
        self.drain()
        total = self.zb[0].astype(F32)
        for i in range(1, 8):
            total = total + self.zb[i].astype(F32)
        c, i, j = self.p.core, self.p.index(self.a), self.p.index(self.b)
        mine = self.fin.at[c, i, j // 2, lax.rem(j, 2)]
        mine[...] = total.astype(BF16)
        for d in range(1, 4):
            o = self.p.other(self.b, d)
            self.put(mine, mine, self.p.peer(self.b, o))

    def step5(self):
        self.drain()
        mine = self.fin.at[self.p.core, self.p.index(self.a)]
        for d in range(1, 4):
            o = self.p.other(self.a, d)
            self.put(mine, mine, self.p.peer(self.a, o))

    def step6(self):
        self.drain()
        mine = self.fin.at[self.p.core]
        self.put(mine, mine, self.p.peer("core", self.p.other("core", 1)))


PART_SHAPES = [
    (2, 4, 2, 2, 24, 128),
    (4, 2, 2, 24, 128),
    (4, 2, 2, 24, 128),
    (3, 2, 2, 24, 128),
    (2, 2, 24, 128),
    (3, 24, 128),
    (8, 24, 128),
    (2, 4, 2, 2, 24, 128),
]
PART_SEMS = 21


class BiasSum:
    axes = ("core", "x", "y", "z")

    def __init__(self, place, slots, send, recv):
        self.p, self.slots, self.send, self.recv = place, slots, send, recv
        self.sem = 0
        self.open = []

    def exchange(self, axis, buf):
        i = self.p.index(axis)
        for d in range(1, self.p.sizes[axis]):
            copy = pltpu.make_async_remote_copy(
                src_ref=buf.at[i],
                dst_ref=buf.at[i],
                send_sem=self.send.at[self.sem],
                recv_sem=self.recv.at[self.sem],
                device_id=self.p.peer(axis, self.p.other(axis, d)),
                device_id_type=MESH,
            )
            self.sem += 1
            copy.start()
            self.open.append(copy)

    def begin(self, level, value):
        axis, buf = self.axes[level], self.slots[level]
        buf[self.p.index(axis)] = value
        self.exchange(axis, buf)

    def finish(self, level):
        for copy in self.open:
            copy.wait()
        self.open = []
        buf = self.slots[level]
        total = buf[0]
        for i in range(1, self.p.sizes[self.axes[level]]):
            total = total + buf[i]
        return total


def kernel(
    frames,
    x_hbm, up_hbm, w1, b1, w2, b2,
    out_hbm, gin_hbm, gw1, gb1, gw2, gb2,
    xin, up, hid, xt, hidt, s1, g2, gh, g1, outb, ginb, w1t, w2t, acc1, acc2, db1, db2,
    *rest,
):
    nb = frames // R
    bufs, rest = rest[: 4 * len(PART_SHAPES)], rest[4 * len(PART_SHAPES) :]
    slots, rest = rest[:4], rest[4:]
    load_sem, out_sem, halo_send, halo_recv, ar_send, ar_recv, bias_send, bias_recv = rest

    place = Place()
    f, r = place.f, place.r
    n = lax.axis_size("frames")
    after = (lax.rem(f + 1, n), r)
    before = (lax.rem(f + n - 1, n), r)

    barrier = pltpu.get_barrier_semaphore()
    peers = [after, before]
    for axis, size in Place.sizes.items():
        for d in range(1, size):
            peers.append(place.peer(axis, place.other(axis, d)))
    for peer in peers:
        pl.semaphore_signal(barrier, inc=1, device_id=peer, device_id_type=MESH)

    tail = 3 * R
    loads = [
        pltpu.make_async_copy(x_hbm.at[pl.ds(frames - tail, tail)], xin.at[pl.ds(H1 + frames - tail, tail)], load_sem.at[0]),
        pltpu.make_async_copy(x_hbm.at[pl.ds(0, frames - tail)], xin.at[pl.ds(H1, frames - tail)], load_sem.at[1]),
        pltpu.make_async_copy(up_hbm, up, load_sem.at[2]),
    ]
    for copy in loads:
        copy.start()

    def halo(k, src, dst, to):
        return pltpu.make_async_remote_copy(
            src_ref=src, dst_ref=dst, send_sem=halo_send.at[k], recv_sem=halo_recv.at[k],
            device_id=to, device_id_type=MESH,
        )

    send_x = halo(0, xin.at[pl.ds(frames, H1)], xin.at[pl.ds(0, H1)], after)
    send_h = halo(1, hid.at[pl.ds(frames, H2)], hid.at[pl.ds(0, H2)], after)
    send_g2 = halo(2, g2.at[pl.ds(0, H2)], g2.at[pl.ds(frames, H2)], before)
    send_g1 = halo(3, g1.at[pl.ds(0, H1)], g1.at[pl.ds(frames, H1)], before)

    for k in range(3):
        w1t[pl.ds(k * C, C), :] = w1[pl.ds(k * C, C), :].T
        w2t[pl.ds(k * C, C), :] = w2[pl.ds(k * C, C), :].T
    acc1[...] = jnp.zeros_like(acc1)
    acc2[...] = jnp.zeros_like(acc2)
    db1[...] = jnp.zeros_like(db1)
    db2[...] = jnp.zeros_like(db2)
    bias1 = b1[...].astype(F32)
    bias2 = b2[...].astype(F32)

    def rows(start, size=R):
        return pl.ds(pl.multiple_of(start, 256), size)

    def block_f1(b):
        t = b * R
        x0 = xin[rows(t + H1), :]
        x1 = xin[rows(t + H1 - D1), :]
        x2 = xin[rows(t), :]
        pre = dot(jnp.concatenate([x0, x1, x2], axis=1), w1[...]) + bias1
        act, slope = gelu_parts(pre)
        h = (x0.astype(F32) + act).astype(BF16)
        hid[rows(t + H2), :] = h
        s1[rows(t), :] = slope
        xt[:, rows(t + H1)] = x0.T
        hidt[:, rows(t + H2)] = h.T

    def block_f2(b):
        t = b * R
        h0 = hid[rows(t + H2), :]
        h1 = hid[rows(t + H2 - D2), :]
        h2 = hid[rows(t), :]
        pre = dot(jnp.concatenate([h0, h1, h2], axis=1), w2[...]) + bias2
        act, slope = gelu_parts(pre)
        outb[rows(t), :] = (h0.astype(F32) + act).astype(BF16)
        g = up[rows(t), :].astype(F32) * slope
        db2[...] += jnp.sum(g.reshape(R // 8, 8, C), axis=0)
        gb = g.astype(BF16)
        g2[rows(t), :] = gb
        for k in range(3):
            acc2[pl.ds(k * C, C), :] += dot(hidt[:, rows(t + H2 - k * D2)], gb)
        out_copy(b).start()

    def block_b2(b):
        t = b * R
        cat = jnp.concatenate([g2[rows(t + k * D2), :] for k in range(3)], axis=1)
        grad = dot(cat, w2t[...]) + up[rows(t), :].astype(F32)
        gh[rows(t), :] = grad
        g = grad * s1[rows(t), :]
        db1[...] += jnp.sum(g.reshape(R // 8, 8, C), axis=0)
        gb = g.astype(BF16)
        g1[rows(t), :] = gb
        for k in range(3):
            acc1[pl.ds(k * C, C), :] += dot(xt[:, rows(t + H1 - k * D1)], gb)

    def block_b1(b):
        t = b * R
        cat = jnp.concatenate([g1[rows(t + k * D1), :] for k in range(3)], axis=1)
        ginb[rows(t), :] = (dot(cat, w1t[...]) + gh[rows(t), :]).astype(BF16)
        gin_copy(b).start()

    def out_copy(b):
        return pltpu.make_async_copy(outb.at[rows(b * R)], out_hbm.at[rows(b * R)], out_sem.at[b])

    def gin_copy(b):
        return pltpu.make_async_copy(ginb.at[rows(b * R)], gin_hbm.at[rows(b * R)], out_sem.at[nb + b])

    def loop(lo, hi, block):
        if hi - lo == 1:
            block(lo)
            return

        def body(b, _):
            block(b)
            return 0

        lax.fori_loop(lo, hi, body, 0)

    def parts_of(layer):
        made = []
        for q, order in enumerate((("x", "y"), ("y", "x"))):
            k = layer * 2 + q
            refs = bufs[k * len(PART_SHAPES) : (k + 1) * len(PART_SHAPES)]
            made.append(Part(place, order, refs, ar_send.at[k], ar_recv.at[k]))
        return made

    def pack(acc, made):
        for q, part in enumerate(made):
            for h in range(2):
                piece = acc[pl.ds(q * 384, 384), pl.ds(h * 128, 128)] * (1.0 / 1024.0)
                part.s0[:, :, :, h] = piece.reshape(2, 4, 2, 24, 128).astype(BF16)

    def unpack(acc, made):
        for q, part in enumerate(made):
            for h in range(2):
                acc[pl.ds(q * 384, 384), pl.ds(h * 128, 128)] = (
                    part.fin[:, :, :, h].astype(F32).reshape(384, 128)
                )

    def run(made, k):
        for part in made:
            part.steps()[k]()

    loads[0].wait()
    loop(nb - 2, nb, block_f1)
    pl.semaphore_wait(barrier, len(peers))
    send_x.start()
    send_h.start()
    loads[1].wait()
    loop(1, nb - 2, block_f1)
    send_x.wait()

    @pl.when(f == 0)
    def _():
        xin[pl.ds(0, H1), :] = jnp.zeros((H1, C), BF16)

    xt[:, pl.ds(0, H1)] = xin[pl.ds(0, H1), :].T
    loop(0, 1, block_f1)
    send_h.wait()

    @pl.when(f == 0)
    def _():
        hid[pl.ds(0, H2), :] = jnp.zeros((H2, C), BF16)

    hidt[:, pl.ds(0, H2)] = hid[pl.ds(0, H2), :].T

    loads[2].wait()
    loop(0, 2, block_f2)
    send_g2.start()
    loop(2, nb, block_f2)
    layer2 = parts_of(1)
    pack(acc2, layer2)
    run(layer2, 0)

    loop(0, 1, block_b2)
    send_g1.start()
    run(layer2, 1)
    loop(1, 3, block_b2)
    run(layer2, 2)
    loop(3, nb - 2, block_b2)
    run(layer2, 3)
    send_g2.wait()

    @pl.when(f == n - 1)
    def _():
        g2[pl.ds(frames, H2), :] = jnp.zeros((H2, C), BF16)

    loop(nb - 2, nb, block_b2)
    layer1 = parts_of(0)
    pack(acc1, layer1)
    run(layer1, 0)
    bias = BiasSum(place, slots, bias_send, bias_recv)
    both = jnp.concatenate(
        [jnp.sum(v[...], axis=0, keepdims=True)[:, h * 128 : (h + 1) * 128] for v in (db2, db1) for h in range(2)]
        + [jnp.zeros((4, 128), F32)],
        axis=0,
    ) * (1.0 / 1024.0)
    bias.begin(0, both)
    run(layer2, 4)
    loop(0, 2, block_b1)
    run(layer1, 1)
    bias.begin(1, bias.finish(0))
    run(layer2, 5)
    loop(2, 5, block_b1)
    run(layer1, 2)
    bias.begin(2, bias.finish(1))
    run(layer2, 6)
    loop(5, nb - 1, block_b1)
    send_g1.wait()

    @pl.when(f == n - 1)
    def _():
        g1[pl.ds(frames, H1), :] = jnp.zeros((H1, C), BF16)

    loop(nb - 1, nb, block_b1)
    run(layer1, 3)
    bias.begin(3, bias.finish(2))
    run(layer2, 7)
    unpack(gw2, layer2)
    run(layer1, 4)
    total = bias.finish(3)
    for h in range(2):
        gb2[:, pl.ds(h * 128, 128)] = total[h : h + 1]
        gb1[:, pl.ds(h * 128, 128)] = total[2 + h : 3 + h]
    run(layer1, 5)
    run(layer1, 6)
    for b in range(nb):
        out_copy(b).wait()
        gin_copy(b).wait()
    run(layer1, 7)
    unpack(gw1, layer1)


def body(inputs, first_layer_weight, first_layer_bias, second_layer_weight, second_layer_bias, upstream):
    _, frames, c = inputs.shape
    any_spec = pl.BlockSpec(memory_space=pl.ANY)
    vmem = pl.BlockSpec(memory_space=pltpu.VMEM)
    nb = frames // R
    scratch = [
        pltpu.VMEM((H1 + frames, C), BF16),
        pltpu.VMEM((frames, C), BF16),
        pltpu.VMEM((H2 + frames, C), BF16),
        pltpu.VMEM((C, H1 + frames), BF16),
        pltpu.VMEM((C, H2 + frames), BF16),
        pltpu.VMEM((frames, C), F32),
        pltpu.VMEM((frames + H2, C), BF16),
        pltpu.VMEM((frames, C), F32),
        pltpu.VMEM((frames + H1, C), BF16),
        pltpu.VMEM((frames, C), BF16),
        pltpu.VMEM((frames, C), BF16),
        pltpu.VMEM((3 * C, C), BF16),
        pltpu.VMEM((3 * C, C), BF16),
        pltpu.VMEM((3 * C, C), F32),
        pltpu.VMEM((3 * C, C), F32),
        pltpu.VMEM((8, C), F32),
        pltpu.VMEM((8, C), F32),
    ]
    scratch += [pltpu.VMEM(shape, BF16) for _ in range(4) for shape in PART_SHAPES]
    scratch += [pltpu.VMEM((k, 8, 128), F32) for k in (2, 4, 4, 8)]
    scratch += [
        pltpu.SemaphoreType.DMA((3,)),
        pltpu.SemaphoreType.DMA((2 * nb,)),
        pltpu.SemaphoreType.DMA((4,)),
        pltpu.SemaphoreType.DMA((4,)),
        pltpu.SemaphoreType.DMA((4, PART_SEMS)),
        pltpu.SemaphoreType.DMA((4, PART_SEMS)),
        pltpu.SemaphoreType.DMA((14,)),
        pltpu.SemaphoreType.DMA((14,)),
    ]
    outs = pl.pallas_call(
        functools.partial(kernel, frames),
        out_shape=[
            jax.ShapeDtypeStruct((frames, c), BF16),
            jax.ShapeDtypeStruct((frames, c), BF16),
            jax.ShapeDtypeStruct((3 * C, C), F32),
            jax.ShapeDtypeStruct((1, C), F32),
            jax.ShapeDtypeStruct((3 * C, C), F32),
            jax.ShapeDtypeStruct((1, C), F32),
        ],
        in_specs=[any_spec, any_spec, vmem, vmem, vmem, vmem],
        out_specs=[any_spec, any_spec, vmem, vmem, vmem, vmem],
        scratch_shapes=scratch,
        compiler_params=pltpu.CompilerParams(
            collective_id=0, has_side_effects=True, vmem_limit_bytes=56 * 1024 * 1024
        ),
    )(
        inputs.reshape(frames, c),
        upstream.reshape(frames, c),
        first_layer_weight.reshape(3 * C, C),
        first_layer_bias.reshape(1, C),
        second_layer_weight.reshape(3 * C, C),
        second_layer_bias.reshape(1, C),
    )
    out, gin, gw1, gb1, gw2, gb2 = outs
    return (
        out.reshape(1, frames, c),
        gin.reshape(1, frames, c),
        gw1.reshape(3, C, C),
        gb1.reshape(C),
        gw2.reshape(3, C, C),
        gb2.reshape(C),
    )


def solution(mesh):
    return jax.shard_map(
        body,
        mesh=mesh,
        in_specs=(P("runs", "frames", None), P(), P(), P(), P(), P("runs", "frames", None)),
        out_specs=(P("runs", "frames", None), P("runs", "frames", None), P(), P(), P(), P()),
        check_vma=False,
    )
```

```python
import functools
import itertools
import math

import jax
import jax.numpy as jnp
from jax import lax
from jax.experimental import pallas as pl
from jax.experimental.pallas import tpu as pltpu
from jax.sharding import PartitionSpec as P

C = 256
D1 = 256
D2 = 512
HX = 1536
HH = 1024
R = 512
F32 = jnp.float32
BF16 = jnp.bfloat16
C0 = math.sqrt(2.0 / math.pi)
C1 = C0 * 0.044715
MESH = pl.DeviceIdType.MESH


def gelu_parts(v):
    v2 = v * v
    t = jnp.tanh(v * (C0 + C1 * v2))
    h = 0.5 * v
    act = h + h * t
    slope = (0.5 + 0.5 * t) + (h * (1.0 - t * t)) * (C0 + (3.0 * C1) * v2)
    return act, slope


def dot(a, b):
    return jnp.dot(a, b, preferred_element_type=F32)


def dot_rows(a, b):
    return lax.dot_general(a, b, (((0,), (0,)), ((), ())), preferred_element_type=F32)


class Place:
    sizes = {"core": 2, "xy": 16, "z": 8}

    def __init__(self):
        self.f = lax.axis_index("frames")
        self.r = lax.axis_index("runs")
        self.core = lax.rem(self.f, 2)
        self.z = self.f // 4
        self.x = lax.rem(self.r, 2) * 2 + lax.rem(self.f // 2, 2)
        self.y = self.r // 2

    def device(self, core, x, y, z):
        return (z * 4 + lax.rem(x, 2) * 2 + core, y * 2 + x // 2)

    def index(self, group):
        return {"core": self.core, "xy": self.x * 4 + self.y, "z": self.z}[group]

    def others(self, group):
        if group == "core":
            o = 1 - self.core
            return [(o, self.device(o, self.x, self.y, self.z))]
        if group == "z":
            found = []
            for d in (4, 3, 5, 2, 6, 1, 7):
                o = lax.rem(self.z + d, 8)
                found.append((o, self.device(self.core, self.x, self.y, o)))
            return found
        steps = [s for s in itertools.product(range(4), range(4)) if any(s)]
        steps.sort(key=lambda s: -sum(min(v, 4 - v) for v in s))
        found = []
        for dx, dy in steps:
            x, y = lax.rem(self.x + dx, 4), lax.rem(self.y + dy, 4)
            found.append((x * 4 + y, self.device(self.core, x, y, self.z)))
        return found


class Sender:
    def __init__(self, place, send, recv):
        self.p, self.send, self.recv = place, send, recv
        self.sem = 0
        self.open = []

    def put(self, src, dst, to):
        copy = pltpu.make_async_remote_copy(
            src_ref=src,
            dst_ref=dst,
            send_sem=self.send.at[self.sem],
            recv_sem=self.recv.at[self.sem],
            device_id=to,
            device_id_type=MESH,
        )
        self.sem += 1
        copy.start()
        self.open.append(copy)

    def drain(self):
        for copy in self.open:
            copy.wait()
        self.open = []


class Part(Sender):
    sems = 1 + 15 + 7 + 15 + 1

    def __init__(self, place, a, b, refs, send, recv):
        super().__init__(place, send, recv)
        self.a, self.b = a, b
        self.s0, self.r0, self.s1, self.r1, self.zb, self.fin = refs

    @staticmethod
    def shapes(a, b):
        n2 = Place.sizes[b]
        inner = (8, 2, 24, 128) if a == "xy" else (8, 24, 256)
        chunk = inner[-2:]
        n1 = Place.sizes[a]
        return [(2,) + inner, inner, inner, (n1 - 1,) + chunk, (n2,) + chunk, (2,) + inner]

    def chunk(self, ref, lead, j):
        where = (j // 2, lax.rem(j, 2)) if self.a == "xy" else (j,)
        return ref.at[lead + where]

    def step0(self):
        for o, to in self.p.others("core"):
            self.put(self.s0.at[o], self.r0, to)

    def step1(self):
        self.drain()
        self.s1[...] = (self.s0[self.p.core].astype(F32) + self.r0[...].astype(F32)).astype(BF16)
        for d, (o, to) in enumerate(self.p.others(self.a)):
            self.put(self.chunk(self.s1, (), o), self.r1.at[d], to)

    def step2(self):
        self.drain()
        total = self.chunk(self.s1, (), self.p.index(self.a))[...].astype(F32)
        for d in range(Place.sizes[self.a] - 1):
            total = total + self.r1[d].astype(F32)
        i = self.p.index(self.b)
        self.zb[i] = total.astype(BF16)
        for o, to in self.p.others(self.b):
            self.put(self.zb.at[i], self.zb.at[i], to)

    def step3(self):
        self.drain()
        total = self.zb[0].astype(F32)
        for i in range(1, Place.sizes[self.b]):
            total = total + self.zb[i].astype(F32)
        mine = self.chunk(self.fin, (self.p.core,), self.p.index(self.a))
        mine[...] = total.astype(BF16)
        for o, to in self.p.others(self.a):
            self.put(mine, mine, to)

    def step4(self):
        self.drain()
        mine = self.fin.at[self.p.core]
        for o, to in self.p.others("core"):
            self.put(mine, mine, to)

    def pack(self, acc, row):
        if self.a == "xy":
            for h in range(2):
                piece = acc[pl.ds(row, 384), pl.ds(h * 128, 128)] * (1.0 / 1024.0)
                self.s0[:, :, h] = piece.reshape(2, 8, 24, 128).astype(BF16)
        else:
            piece = acc[pl.ds(row, 384), :] * (1.0 / 1024.0)
            self.s0[...] = piece.reshape(2, 8, 24, 256).astype(BF16)

    def unpack(self, out, row):
        if self.a == "xy":
            for h in range(2):
                out[pl.ds(row, 384), pl.ds(h * 128, 128)] = self.fin[:, :, h].astype(F32).reshape(384, 128)
        else:
            out[pl.ds(row, 384), :] = self.fin[...].astype(F32).reshape(384, 256)


class Layer:
    groups = (("xy", "z"), ("z", "xy"))

    def __init__(self, place, refs, send, recv):
        self.parts = []
        for q, (a, b) in enumerate(self.groups):
            self.parts.append(Part(place, a, b, refs[q * 6 : q * 6 + 6], send.at[q], recv.at[q]))

    def begin(self, acc):
        for q, part in enumerate(self.parts):
            part.pack(acc, q * 384)
            part.step0()

    def step(self, k):
        for part in self.parts:
            getattr(part, "step%d" % k)()

    def end(self, out):
        for q, part in enumerate(self.parts):
            part.drain()
            part.unpack(out, q * 384)


class BiasSum(Sender):
    groups = ("core", "xy", "z")

    def __init__(self, place, slots, send, recv):
        super().__init__(place, send, recv)
        self.slots = slots

    def begin(self, level, value):
        group, buf = self.groups[level], self.slots[level]
        i = self.p.index(group)
        buf[i] = value
        for o, to in self.p.others(group):
            self.put(buf.at[i], buf.at[i], to)

    def finish(self, level):
        self.drain()
        buf = self.slots[level]
        total = buf[0]
        for i in range(1, Place.sizes[self.groups[level]]):
            total = total + buf[i]
        return total


def kernel(
    frames,
    x_hbm, up_hbm, w1_hbm, b1, w2_hbm, b2,
    out_hbm, gin_hbm, gw1, gb1, gw2, gb2,
    xin, xc, up, hid, s1, g2, gh, g1, outb, ginb, pout, pin, tout, tin,
    w1, w2, w1t, w2t, acc1, acc2, db1, db2,
    *rest,
):
    nb = frames // R
    own = nb - 2
    bufs, rest = rest[:24], rest[24:]
    slots, rest = rest[:3], rest[3:]
    load_sem, out_sem, halo_send, halo_recv, ar_send, ar_recv, bias_send, bias_recv = rest

    place = Place()
    f, r = place.f, place.r
    n = lax.axis_size("frames")
    after = (lax.rem(f + 1, n), r)
    before = (lax.rem(f + n - 1, n), r)

    barrier = pltpu.get_barrier_semaphore()
    peers = [after, before] + [to for g in Place.sizes for _, to in place.others(g)]
    for peer in peers:
        pl.semaphore_signal(barrier, inc=1, device_id=peer, device_id_type=MESH)

    tail = 3 * R
    loads = [
        pltpu.make_async_copy(w1_hbm, w1, load_sem.at[0]),
        pltpu.make_async_copy(x_hbm.at[pl.ds(frames - tail, tail)], xin.at[pl.ds(HX + frames - tail, tail)], load_sem.at[1]),
        pltpu.make_async_copy(x_hbm.at[pl.ds(0, frames - tail)], xin.at[pl.ds(HX, frames - tail)], load_sem.at[2]),
        pltpu.make_async_copy(w2_hbm, w2, load_sem.at[3]),
        pltpu.make_async_copy(up_hbm, up, load_sem.at[4]),
    ]
    for copy in loads:
        copy.start()

    def halo(k, src, dst, to):
        return pltpu.make_async_remote_copy(
            src_ref=src, dst_ref=dst, send_sem=halo_send.at[k], recv_sem=halo_recv.at[k],
            device_id=to, device_id_type=MESH,
        )

    send_x1 = halo(0, xin.at[pl.ds(HX + frames - 1024, 1024)], xin.at[pl.ds(HX - 1024, 1024)], after)
    send_x2 = halo(1, xin.at[pl.ds(HX + frames - HX, HX - 1024)], xin.at[pl.ds(0, HX - 1024)], after)
    send_p = halo(2, pout, pin, after)
    send_g1 = halo(3, g1.at[pl.ds(0, 2 * D1)], g1.at[pl.ds(HH + own * R, 2 * D1)], before)
    send_t = halo(4, tout, tin, before)

    g2[pl.ds(0, HH), :] = jnp.zeros((HH, C), BF16)
    g2[pl.ds(HH + frames, HH), :] = jnp.zeros((HH, C), BF16)
    db1[...] = jnp.zeros_like(db1)
    db2[...] = jnp.zeros_like(db2)
    bias1 = b1[...].astype(F32).reshape(1, C)
    bias2 = b2[...].astype(F32).reshape(1, C)
    inner = jnp.where(f == 0, 0.0, 1.0).astype(F32)

    def rows(start, size=R):
        return pl.ds(start if isinstance(start, int) else pl.multiple_of(start, 256), size)

    def forward1(t, src, base, keep):
        x0 = src[rows(base + t), :]
        x1 = src[rows(base + t - D1), :]
        x2 = src[rows(base + t - 2 * D1), :]
        pre = dot(jnp.concatenate([x0, x1, x2], axis=1), w1[...]) + bias1
        act, slope = gelu_parts(pre)
        h = x0.astype(F32) + act
        hid[rows(t + HH), :] = (h if keep is None else h * keep).astype(BF16)
        s1[rows(t + HH), :] = slope

    def block_f1(b):
        forward1(b * R, xin, HX, None)

    def block_f2(b):
        t = b * R
        h = [hid[rows(t + HH - k * D2), :] for k in range(3)]
        pre = dot(jnp.concatenate(h, axis=1), w2[...]) + bias2
        act, slope = gelu_parts(pre)
        outb[rows(t), :] = (h[0].astype(F32) + act).astype(BF16)
        g = up[rows(t), :].astype(F32) * slope
        db2[...] += jnp.sum(g.reshape(R // 8, 8, C), axis=0)
        g2[rows(t + HH), :] = g.astype(BF16)
        out_copy(b).start()

    def hidden_terms(t):
        cat = jnp.concatenate([g2[rows(t + HH + k * D2), :] for k in range(3)], axis=1)
        return dot(cat, w2t[...])

    def backward2(t, grad):
        gh[rows(t + HH), :] = grad
        g = grad * s1[rows(t + HH), :]
        db1[...] += jnp.sum(g.reshape(R // 8, 8, C), axis=0)
        g1[rows(t + HH), :] = g.astype(BF16)

    def block_b2(b):
        t = b * R
        backward2(t, hidden_terms(t) + up[rows(t), :].astype(F32))

    def block_p(b):
        t = b * R
        pout[rows(t - own * R), :] = (hidden_terms(t) + up[rows(t), :].astype(F32)).astype(BF16)

    def block_b2_before(b):
        t = b * R
        backward2(t, pin[rows(t + HH), :].astype(F32) + inner * hidden_terms(t))

    def block_b1(b):
        t = b * R
        cat = jnp.concatenate([g1[rows(t + HH + k * D1), :] for k in range(3)], axis=1)
        ginb[rows(t), :] = (dot(cat, w1t[...]) + gh[rows(t + HH), :]).astype(BF16)
        gin_copy(b).start()

    def grad2(start, size, first=False):
        lhs = jnp.concatenate([hid[rows(start + HH - k * D2, size), :] for k in range(3)], axis=1)
        part = dot_rows(lhs, g2[rows(start + HH, size), :])
        acc2[...] = part if first else acc2[...] + part

    def grad1(start, size, first=False, src=None, base=HX):
        src = xin if src is None else src
        lhs = jnp.concatenate([src[rows(start + base - k * D1, size), :] for k in range(3)], axis=1)
        part = dot_rows(lhs, g1[rows(start + HH, size), :])
        acc1[...] = part if first else acc1[...] + part

    def out_copy(b):
        return pltpu.make_async_copy(outb.at[rows(b * R)], out_hbm.at[rows(b * R)], out_sem.at[b])

    def gin_copy(b):
        return pltpu.make_async_copy(ginb.at[rows(b * R)], gin_hbm.at[rows(b * R)], out_sem.at[nb + b])

    tail_copy = pltpu.make_async_copy(tin, gin_hbm.at[pl.ds(own * R, HH)], out_sem.at[nb + own])

    def loop(lo, hi, block):
        if hi - lo == 1:
            block(lo)
            return

        def body(b, _):
            block(b)
            return 0

        lax.fori_loop(lo, hi, body, 0)

    layer1 = Layer(place, bufs[:12], ar_send.at[0], ar_recv.at[0])
    layer2 = Layer(place, bufs[12:], ar_send.at[1], ar_recv.at[1])

    loads[0].wait()
    loads[1].wait()
    loop(nb - 2, nb, block_f1)
    pl.semaphore_wait(barrier, len(peers))
    send_x1.start()
    send_x2.start()
    loads[2].wait()
    loop(1, nb - 2, block_f1)
    loads[3].wait()
    loads[4].wait()
    for k in range(3):
        w1t[pl.ds(k * C, C), :] = w1[pl.ds(k * C, C), :].T
        w2t[pl.ds(k * C, C), :] = w2[pl.ds(k * C, C), :].T
    loop(3, nb, block_f2)
    loop(own, nb, block_p)
    send_p.start()
    loop(3, own, block_b2)
    grad2(frames - 1024, 1024, True)
    grad2(frames - 2048, 1024)
    grad1(own * R - 1024, 1024, True)
    grad1(own * R - 1536, 512)

    send_x1.wait()
    xc[pl.ds(0, R), :] = (xin[pl.ds(HX - R, R), :].astype(F32) * inner).astype(BF16)
    xc[pl.ds(R, R), :] = xin[pl.ds(HX, R), :]
    forward1(0, xc, R, None)
    forward1(-R, xin, HX, inner)
    loop(1, 3, block_f2)
    send_x2.wait()
    forward1(-2 * R, xin, HX, inner)
    loop(0, 1, block_f2)
    grad2(1024, 1024)
    grad2(0, 1024)
    layer2.begin(acc2)
    loop(0, 3, block_b2)
    layer2.step(1)
    grad1(0, R, False, xc, R)
    grad1(R, 1024)
    send_p.wait()
    block_b2_before(-2)
    send_g1.start()
    block_b2_before(-1)
    grad1(-1024, 1024)
    layer1.begin(acc1)
    bias = BiasSum(place, slots, bias_send, bias_recv)
    both = jnp.concatenate(
        [jnp.sum(v[...], axis=0, keepdims=True)[:, h * 128 : (h + 1) * 128] for v in (db2, db1) for h in range(2)]
        + [jnp.zeros((4, 128), F32)],
        axis=0,
    ) * (1.0 / 1024.0)
    bias.begin(0, both)
    layer2.step(2)

    cat = jnp.concatenate([g1[pl.ds(k * D1, R), :] for k in range(3)], axis=1)
    tout[pl.ds(0, R), :] = (dot(cat, w1t[...]) + gh[pl.ds(0, R), :]).astype(BF16)
    edge = (g1[pl.ds(HH, R), :].astype(F32) * inner).astype(BF16)
    cat = jnp.concatenate(
        [
            g1[pl.ds(R, R), :],
            jnp.concatenate([g1[pl.ds(R + D1, D1), :], edge[:D1]], axis=0),
            edge,
        ],
        axis=1,
    )
    tout[pl.ds(R, R), :] = (dot(cat, w1t[...]) + gh[pl.ds(R, R), :]).astype(BF16)
    layer1.step(1)
    bias.begin(1, bias.finish(0))
    send_t.start()
    loop(0, own - 1, block_b1)
    layer2.step(3)
    layer1.step(2)
    bias.begin(2, bias.finish(1))
    send_g1.wait()
    loop(own - 1, own, block_b1)
    layer2.step(4)
    layer1.step(3)
    total = bias.finish(2)
    for h in range(2):
        gb2[:, pl.ds(h * 128, 128)] = total[h : h + 1]
        gb1[:, pl.ds(h * 128, 128)] = total[2 + h : 3 + h]
    layer2.end(gw2)
    send_t.wait()
    tail_copy.start()
    layer1.step(4)
    for b in range(nb):
        out_copy(b).wait()
    for b in range(own):
        gin_copy(b).wait()
    tail_copy.wait()
    layer1.end(gw1)


def body(inputs, first_layer_weight, first_layer_bias, second_layer_weight, second_layer_bias, upstream):
    _, frames, c = inputs.shape
    any_spec = pl.BlockSpec(memory_space=pl.ANY)
    vmem = pl.BlockSpec(memory_space=pltpu.VMEM)
    nb = frames // R
    scratch = [
        pltpu.VMEM((HX + frames, C), BF16),
        pltpu.VMEM((2 * R, C), BF16),
        pltpu.VMEM((frames, C), BF16),
        pltpu.VMEM((HH + frames, C), BF16),
        pltpu.VMEM((HH + frames, C), F32),
        pltpu.VMEM((HH + frames + HH, C), BF16),
        pltpu.VMEM((frames, C), F32),
        pltpu.VMEM((frames + 2 * D1, C), BF16),
        pltpu.VMEM((frames, C), BF16),
        pltpu.VMEM((frames - HH, C), BF16),
        pltpu.VMEM((HH, C), BF16),
        pltpu.VMEM((HH, C), BF16),
        pltpu.VMEM((HH, C), BF16),
        pltpu.VMEM((HH, C), BF16),
        pltpu.VMEM((3 * C, C), BF16),
        pltpu.VMEM((3 * C, C), BF16),
        pltpu.VMEM((3 * C, C), BF16),
        pltpu.VMEM((3 * C, C), BF16),
        pltpu.VMEM((3 * C, C), F32),
        pltpu.VMEM((3 * C, C), F32),
        pltpu.VMEM((8, C), F32),
        pltpu.VMEM((8, C), F32),
    ]
    scratch += [pltpu.VMEM(s, BF16) for _ in range(2) for a, b in Layer.groups for s in Part.shapes(a, b)]
    scratch += [pltpu.VMEM((k, 8, 128), F32) for k in (2, 16, 8)]
    scratch += [
        pltpu.SemaphoreType.DMA((5,)),
        pltpu.SemaphoreType.DMA((2 * nb,)),
        pltpu.SemaphoreType.DMA((5,)),
        pltpu.SemaphoreType.DMA((5,)),
        pltpu.SemaphoreType.DMA((2, 2, Part.sems)),
        pltpu.SemaphoreType.DMA((2, 2, Part.sems)),
        pltpu.SemaphoreType.DMA((23,)),
        pltpu.SemaphoreType.DMA((23,)),
    ]
    outs = pl.pallas_call(
        functools.partial(kernel, frames),
        out_shape=[
            jax.ShapeDtypeStruct((frames, c), BF16),
            jax.ShapeDtypeStruct((frames, c), BF16),
            jax.ShapeDtypeStruct((3 * C, C), F32),
            jax.ShapeDtypeStruct((1, C), F32),
            jax.ShapeDtypeStruct((3 * C, C), F32),
            jax.ShapeDtypeStruct((1, C), F32),
        ],
        in_specs=[any_spec, any_spec, any_spec, vmem, any_spec, vmem],
        out_specs=[any_spec, any_spec, vmem, vmem, vmem, vmem],
        scratch_shapes=scratch,
        compiler_params=pltpu.CompilerParams(
            collective_id=0, has_side_effects=True, vmem_limit_bytes=56 * 1024 * 1024
        ),
    )(
        inputs.reshape(frames, c),
        upstream.reshape(frames, c),
        first_layer_weight.reshape(3 * C, C),
        first_layer_bias,
        second_layer_weight.reshape(3 * C, C),
        second_layer_bias,
    )
    out, gin, gw1, gb1, gw2, gb2 = outs
    return (
        out.reshape(1, frames, c),
        gin.reshape(1, frames, c),
        gw1.reshape(3, C, C),
        gb1.reshape(C),
        gw2.reshape(3, C, C),
        gb2.reshape(C),
    )


def solution(mesh):
    return jax.shard_map(
        body,
        mesh=mesh,
        in_specs=(P("runs", "frames", None), P(), P(), P(), P(), P("runs", "frames", None)),
        out_specs=(P("runs", "frames", None), P("runs", "frames", None), P(), P(), P(), P()),
        check_vma=False,
    )
```

```python
import functools
import itertools
import math

import jax
import jax.numpy as jnp
from jax import lax
from jax.experimental import pallas as pl
from jax.experimental.pallas import tpu as pltpu
from jax.sharding import PartitionSpec as P

C = 256
D1 = 256
D2 = 512
HX = 1536
HH = 1024
R = 512
F32 = jnp.float32
BF16 = jnp.bfloat16
C0 = math.sqrt(2.0 / math.pi)
C1 = C0 * 0.044715
MESH = pl.DeviceIdType.MESH


def gelu_parts(v):
    v2 = v * v
    t = jnp.tanh(v * (C0 + C1 * v2))
    h = 0.5 * v
    act = h + h * t
    slope = (0.5 + 0.5 * t) + (h * (1.0 - t * t)) * (C0 + (3.0 * C1) * v2)
    return act, slope


def dot(a, b):
    return jnp.dot(a, b, preferred_element_type=F32)


def dot_rows(a, b):
    return lax.dot_general(a, b, (((0,), (0,)), ((), ())), preferred_element_type=F32)


class Place:
    sizes = {"core": 2, "xy": 16, "z": 8}

    def __init__(self):
        self.f = lax.axis_index("frames")
        self.r = lax.axis_index("runs")
        self.core = lax.rem(self.f, 2)
        self.z = self.f // 4
        self.x = lax.rem(self.r, 2) * 2 + lax.rem(self.f // 2, 2)
        self.y = self.r // 2

    def device(self, core, x, y, z):
        return (z * 4 + lax.rem(x, 2) * 2 + core, y * 2 + x // 2)

    def index(self, group):
        return {"core": self.core, "xy": self.x * 4 + self.y, "z": self.z}[group]

    def others(self, group):
        if group == "core":
            o = 1 - self.core
            return [(o, self.device(o, self.x, self.y, self.z))]
        if group == "z":
            found = []
            for d in (4, 3, 5, 2, 6, 1, 7):
                o = lax.rem(self.z + d, 8)
                found.append((o, self.device(self.core, self.x, self.y, o)))
            return found
        steps = [s for s in itertools.product(range(4), range(4)) if any(s)]
        steps.sort(key=lambda s: -sum(min(v, 4 - v) for v in s))
        found = []
        for dx, dy in steps:
            x, y = lax.rem(self.x + dx, 4), lax.rem(self.y + dy, 4)
            found.append((x * 4 + y, self.device(self.core, x, y, self.z)))
        return found


class Sender:
    def __init__(self, place, send, recv):
        self.p, self.send, self.recv = place, send, recv
        self.sem = 0
        self.open = []
        self.sent = []

    def put(self, src, dst, to):
        copy = pltpu.make_async_remote_copy(
            src_ref=src,
            dst_ref=dst,
            send_sem=self.send.at[self.sem],
            recv_sem=self.recv.at[self.sem],
            device_id=to,
            device_id_type=MESH,
        )
        self.sem += 1
        copy.start()
        self.open.append(copy)
        self.sent.append(copy)

    def drain(self):
        for copy in self.open:
            copy.wait_recv()
        self.open = []

    def finish_sends(self):
        for copy in self.sent:
            copy.wait_send()


class Part(Sender):
    sems = 1 + 15 + 7 + 15 + 1

    def __init__(self, place, a, b, refs, send, recv):
        super().__init__(place, send, recv)
        self.a, self.b = a, b
        self.s0, self.r0, self.s1, self.r1, self.zb, self.fin = refs

    @staticmethod
    def shapes(a, b):
        n2 = Place.sizes[b]
        inner = (8, 2, 24, 128) if a == "xy" else (8, 24, 256)
        chunk = inner[-2:]
        n1 = Place.sizes[a]
        return [(2,) + inner, inner, inner, (n1 - 1,) + chunk, (n2,) + chunk], (2,) + inner

    def chunk(self, ref, lead, j):
        where = (j // 2, lax.rem(j, 2)) if self.a == "xy" else (j,)
        return ref.at[lead + where]

    def step0(self):
        for o, to in self.p.others("core"):
            self.put(self.s0.at[o], self.r0, to)

    def step1(self):
        self.drain()
        self.s1[...] = (self.s0[self.p.core].astype(F32) + self.r0[...].astype(F32)).astype(BF16)
        for d, (o, to) in enumerate(self.p.others(self.a)):
            self.put(self.chunk(self.s1, (), o), self.r1.at[d], to)

    def step2(self):
        self.drain()
        total = self.chunk(self.s1, (), self.p.index(self.a))[...].astype(F32)
        for d in range(Place.sizes[self.a] - 1):
            total = total + self.r1[d].astype(F32)
        i = self.p.index(self.b)
        self.zb[i] = total.astype(BF16)
        for o, to in self.p.others(self.b):
            self.put(self.zb.at[i], self.zb.at[i], to)

    def step3(self):
        self.drain()
        total = self.zb[0].astype(F32)
        for i in range(1, Place.sizes[self.b]):
            total = total + self.zb[i].astype(F32)
        mine = self.chunk(self.fin, (self.p.core,), self.p.index(self.a))
        mine[...] = total.astype(BF16)
        for o, to in self.p.others(self.a):
            self.put(mine, mine, to)

    def step4(self):
        self.drain()
        mine = self.fin.at[self.p.core]
        for o, to in self.p.others("core"):
            self.put(mine, mine, to)

    def pack(self, acc, row):
        if self.a == "xy":
            for h in range(2):
                piece = acc[pl.ds(row, 384), pl.ds(h * 128, 128)] * (1.0 / 1024.0)
                self.s0[:, :, h] = piece.reshape(2, 8, 24, 128).astype(BF16)
        else:
            piece = acc[pl.ds(row, 384), :] * (1.0 / 1024.0)
            self.s0[...] = piece.reshape(2, 8, 24, 256).astype(BF16)


class Layer:
    groups = (("xy", "z"), ("z", "xy"))

    def __init__(self, place, refs, fins, send, recv):
        self.parts = []
        for q, (a, b) in enumerate(self.groups):
            own = tuple(refs[q * 5 : q * 5 + 5]) + (fins[q],)
            self.parts.append(Part(place, a, b, own, send.at[q], recv.at[q]))

    def begin(self, acc):
        for q, part in enumerate(self.parts):
            part.pack(acc, q * 384)
            part.step0()

    def step(self, k):
        for part in self.parts:
            getattr(part, "step%d" % k)()

    def end(self):
        for part in self.parts:
            part.drain()

    def finish_sends(self):
        for part in self.parts:
            part.finish_sends()


class BiasSum(Sender):
    groups = ("core", "xy", "z")

    def __init__(self, place, slots, send, recv):
        super().__init__(place, send, recv)
        self.slots = slots

    def begin(self, level, value):
        group, buf = self.groups[level], self.slots[level]
        i = self.p.index(group)
        buf[i] = value
        for o, to in self.p.others(group):
            self.put(buf.at[i], buf.at[i], to)

    def finish(self, level):
        self.drain()
        buf = self.slots[level]
        total = buf[0]
        for i in range(1, Place.sizes[self.groups[level]]):
            total = total + buf[i]
        return total


def kernel(
    frames,
    x_hbm, up_hbm, w1_hbm, b1, w2_hbm, b2,
    outb, ginb, fin1a, fin1b, fin2a, fin2b, biases,
    xin, xc, up, hid, s1, g2, gh, g1, pout, pin, tout,
    w1, w2, w1t, w2t, acc1, acc2, db1, db2,
    *rest,
):
    nb = frames // R
    own = nb - 2
    bufs, rest = rest[:20], rest[20:]
    slots, rest = rest[:3], rest[3:]
    load_sem, halo_send, halo_recv, ar_send, ar_recv, bias_send, bias_recv = rest

    place = Place()
    f, r = place.f, place.r
    n = lax.axis_size("frames")
    after = (lax.rem(f + 1, n), r)
    before = (lax.rem(f + n - 1, n), r)

    barrier = pltpu.get_barrier_semaphore()
    peers = [after, before] + [to for g in Place.sizes for _, to in place.others(g)]
    for peer in peers:
        pl.semaphore_signal(barrier, inc=1, device_id=peer, device_id_type=MESH)

    tail = 3 * R
    loads = [
        pltpu.make_async_copy(w1_hbm, w1, load_sem.at[0]),
        pltpu.make_async_copy(x_hbm.at[pl.ds(frames - tail, tail)], xin.at[pl.ds(HX + frames - tail, tail)], load_sem.at[1]),
        pltpu.make_async_copy(x_hbm.at[pl.ds(0, frames - tail)], xin.at[pl.ds(HX, frames - tail)], load_sem.at[2]),
        pltpu.make_async_copy(w2_hbm, w2, load_sem.at[3]),
        pltpu.make_async_copy(up_hbm, up, load_sem.at[4]),
    ]
    for copy in loads:
        copy.start()

    def halo(k, src, dst, to):
        return pltpu.make_async_remote_copy(
            src_ref=src, dst_ref=dst, send_sem=halo_send.at[k], recv_sem=halo_recv.at[k],
            device_id=to, device_id_type=MESH,
        )

    send_x1 = halo(0, xin.at[pl.ds(HX + frames - 1024, 1024)], xin.at[pl.ds(HX - 1024, 1024)], after)
    send_x2 = halo(1, xin.at[pl.ds(HX + frames - HX, HX - 1024)], xin.at[pl.ds(0, HX - 1024)], after)
    send_p = halo(2, pout, pin, after)
    send_g1 = halo(3, g1.at[pl.ds(0, 2 * D1)], g1.at[pl.ds(HH + own * R, 2 * D1)], before)
    send_t = halo(4, tout, ginb.at[pl.ds(own * R, HH)], before)

    g2[pl.ds(0, HH), :] = jnp.zeros((HH, C), BF16)
    g2[pl.ds(HH + frames, HH), :] = jnp.zeros((HH, C), BF16)
    db1[...] = jnp.zeros_like(db1)
    db2[...] = jnp.zeros_like(db2)
    bias1 = b1[...].astype(F32).reshape(1, C)
    bias2 = b2[...].astype(F32).reshape(1, C)
    inner = jnp.where(f == 0, 0.0, 1.0).astype(F32)

    def rows(start, size=R):
        return pl.ds(start if isinstance(start, int) else pl.multiple_of(start, 256), size)

    def forward1(t, src, base, keep):
        x0 = src[rows(base + t), :]
        x1 = src[rows(base + t - D1), :]
        x2 = src[rows(base + t - 2 * D1), :]
        pre = dot(jnp.concatenate([x0, x1, x2], axis=1), w1[...]) + bias1
        act, slope = gelu_parts(pre)
        h = x0.astype(F32) + act
        hid[rows(t + HH), :] = (h if keep is None else h * keep).astype(BF16)
        s1[rows(t + HH), :] = slope

    def block_f1(b):
        forward1(b * R, xin, HX, None)

    def block_f2(b):
        t = b * R
        h = [hid[rows(t + HH - k * D2), :] for k in range(3)]
        pre = dot(jnp.concatenate(h, axis=1), w2[...]) + bias2
        act, slope = gelu_parts(pre)
        outb[rows(t), :] = (h[0].astype(F32) + act).astype(BF16)
        g = up[rows(t), :].astype(F32) * slope
        db2[...] += jnp.sum(g.reshape(R // 8, 8, C), axis=0)
        g2[rows(t + HH), :] = g.astype(BF16)

    def hidden_terms(t):
        cat = jnp.concatenate([g2[rows(t + HH + k * D2), :] for k in range(3)], axis=1)
        return dot(cat, w2t[...])

    def backward2(t, grad):
        gh[rows(t + HH), :] = grad
        g = grad * s1[rows(t + HH), :]
        db1[...] += jnp.sum(g.reshape(R // 8, 8, C), axis=0)
        g1[rows(t + HH), :] = g.astype(BF16)

    def block_b2(b):
        t = b * R
        backward2(t, hidden_terms(t) + up[rows(t), :].astype(F32))

    def block_p(b):
        t = b * R
        pout[rows(t - own * R), :] = (hidden_terms(t) + up[rows(t), :].astype(F32)).astype(BF16)

    def block_b2_before(b):
        t = b * R
        backward2(t, pin[rows(t + HH), :].astype(F32) + inner * hidden_terms(t))

    def block_b1(b):
        t = b * R
        cat = jnp.concatenate([g1[rows(t + HH + k * D1), :] for k in range(3)], axis=1)
        ginb[rows(t), :] = (dot(cat, w1t[...]) + gh[rows(t + HH), :]).astype(BF16)

    def grad2(start, size, first=False):
        lhs = jnp.concatenate([hid[rows(start + HH - k * D2, size), :] for k in range(3)], axis=1)
        part = dot_rows(lhs, g2[rows(start + HH, size), :])
        acc2[...] = part if first else acc2[...] + part

    def grad1(start, size, first=False, src=None, base=HX):
        src = xin if src is None else src
        lhs = jnp.concatenate([src[rows(start + base - k * D1, size), :] for k in range(3)], axis=1)
        part = dot_rows(lhs, g1[rows(start + HH, size), :])
        acc1[...] = part if first else acc1[...] + part

    def loop(lo, hi, block):
        if hi - lo == 1:
            block(lo)
            return

        def body(b, _):
            block(b)
            return 0

        lax.fori_loop(lo, hi, body, 0)

    layer1 = Layer(place, bufs[:10], (fin1a, fin1b), ar_send.at[0], ar_recv.at[0])
    layer2 = Layer(place, bufs[10:], (fin2a, fin2b), ar_send.at[1], ar_recv.at[1])
    bias = BiasSum(place, slots, bias_send, bias_recv)

    loads[0].wait()
    for k in range(3):
        w1t[pl.ds(k * C, C), :] = w1[pl.ds(k * C, C), :].T
    loads[1].wait()
    loop(nb - 2, nb, block_f1)
    loads[2].wait()
    loop(1, nb - 2, block_f1)
    loads[3].wait()
    for k in range(3):
        w2t[pl.ds(k * C, C), :] = w2[pl.ds(k * C, C), :].T
    loads[4].wait()
    pl.semaphore_wait(barrier, len(peers))
    send_x1.start()
    send_x2.start()
    loop(own, nb, block_f2)
    loop(own, nb, block_p)
    send_p.start()
    loop(3, own, block_f2)
    loop(3, own, block_b2)
    grad2(frames - 1024, 1024, True)
    grad2(frames - 2048, 1024)
    grad1(own * R - 1024, 1024, True)
    grad1(own * R - 1536, 512)

    send_x1.wait_recv()
    xc[pl.ds(0, R), :] = (xin[pl.ds(HX - R, R), :].astype(F32) * inner).astype(BF16)
    xc[pl.ds(R, R), :] = xin[pl.ds(HX, R), :]
    forward1(0, xc, R, None)
    forward1(-R, xin, HX, inner)
    loop(1, 3, block_f2)
    send_x2.wait_recv()
    forward1(-2 * R, xin, HX, inner)
    loop(0, 1, block_f2)
    loop(0, 3, block_b2)
    grad2(1024, 1024)
    grad2(0, 1024)
    layer2.begin(acc2)
    grad1(0, R, False, xc, R)
    grad1(R, 1024)
    layer2.step(1)
    send_p.wait_recv()
    block_b2_before(-2)
    send_g1.start()
    block_b2_before(-1)
    grad1(-1024, 1024)
    layer1.begin(acc1)
    both = jnp.concatenate(
        [jnp.sum(v[...], axis=0, keepdims=True)[:, h * 128 : (h + 1) * 128] for v in (db2, db1) for h in range(2)]
        + [jnp.zeros((4, 128), F32)],
        axis=0,
    ) * (1.0 / 1024.0)
    bias.begin(0, both)

    cat = jnp.concatenate([g1[pl.ds(k * D1, R), :] for k in range(3)], axis=1)
    tout[pl.ds(0, R), :] = (dot(cat, w1t[...]) + gh[pl.ds(0, R), :]).astype(BF16)
    edge = (g1[pl.ds(HH, R), :].astype(F32) * inner).astype(BF16)
    cat = jnp.concatenate(
        [
            g1[pl.ds(R, R), :],
            jnp.concatenate([g1[pl.ds(R + D1, D1), :], edge[:D1]], axis=0),
            edge,
        ],
        axis=1,
    )
    tout[pl.ds(R, R), :] = (dot(cat, w1t[...]) + gh[pl.ds(R, R), :]).astype(BF16)
    send_t.start()
    layer1.step(1)
    bias.begin(1, bias.finish(0))
    loop(0, own - 1, block_b1)
    layer2.step(2)
    send_g1.wait_recv()
    loop(own - 1, own, block_b1)
    layer1.step(2)
    bias.begin(2, bias.finish(1))
    layer2.step(3)
    layer1.step(3)
    biases[...] = bias.finish(2)
    layer2.step(4)
    layer1.step(4)
    layer2.end()
    send_t.wait_recv()
    for copy in (send_x1, send_x2, send_p, send_g1, send_t):
        copy.wait_send()
    bias.finish_sends()
    layer2.finish_sends()
    layer1.finish_sends()
    layer1.end()


def write_kernel(outb, ginb, fin1a, fin1b, fin2a, fin2b, biases, out, gin, gw1, gb1, gw2, gb2, wide1, wide2, sem):
    copies = [pltpu.make_async_copy(outb, out, sem.at[0]), pltpu.make_async_copy(ginb, gin, sem.at[1])]
    for copy in copies:
        copy.start()
    for k, (a, b, wide, dst) in enumerate(((fin1a, fin1b, wide1, gw1), (fin2a, fin2b, wide2, gw2))):
        for h in range(2):
            wide[pl.ds(0, 384), pl.ds(h * 128, 128)] = a[:, :, h].astype(F32).reshape(384, 128)
        wide[pl.ds(384, 384), :] = b[...].astype(F32).reshape(384, 256)
        copies.append(pltpu.make_async_copy(wide, dst, sem.at[2 + k]))
        copies[-1].start()
    for h in range(2):
        gb2[:, pl.ds(h * 128, 128)] = biases[pl.ds(h, 1), :]
        gb1[:, pl.ds(h * 128, 128)] = biases[pl.ds(2 + h, 1), :]
    for copy in copies:
        copy.wait()


def body(inputs, first_layer_weight, first_layer_bias, second_layer_weight, second_layer_bias, upstream):
    _, frames, c = inputs.shape
    any_spec = pl.BlockSpec(memory_space=pl.ANY)
    vmem = pl.BlockSpec(memory_space=pltpu.VMEM)
    nb = frames // R
    scratch = [
        pltpu.VMEM((HX + frames, C), BF16),
        pltpu.VMEM((2 * R, C), BF16),
        pltpu.VMEM((frames, C), BF16),
        pltpu.VMEM((HH + frames, C), BF16),
        pltpu.VMEM((HH + frames, C), F32),
        pltpu.VMEM((HH + frames + HH, C), BF16),
        pltpu.VMEM((frames, C), F32),
        pltpu.VMEM((frames + 2 * D1, C), BF16),
        pltpu.VMEM((HH, C), BF16),
        pltpu.VMEM((HH, C), BF16),
        pltpu.VMEM((HH, C), BF16),
        pltpu.VMEM((3 * C, C), BF16),
        pltpu.VMEM((3 * C, C), BF16),
        pltpu.VMEM((3 * C, C), BF16),
        pltpu.VMEM((3 * C, C), BF16),
        pltpu.VMEM((3 * C, C), F32),
        pltpu.VMEM((3 * C, C), F32),
        pltpu.VMEM((8, C), F32),
        pltpu.VMEM((8, C), F32),
    ]
    scratch += [pltpu.VMEM(s, BF16) for _ in range(2) for a, b in Layer.groups for s in Part.shapes(a, b)[0]]
    fins = [Part.shapes(a, b)[1] for _ in range(2) for a, b in Layer.groups]
    scratch += [pltpu.VMEM((k, 8, 128), F32) for k in (2, 16, 8)]
    scratch += [
        pltpu.SemaphoreType.DMA((5,)),
        pltpu.SemaphoreType.DMA((5,)),
        pltpu.SemaphoreType.DMA((5,)),
        pltpu.SemaphoreType.DMA((2, 2, Part.sems)),
        pltpu.SemaphoreType.DMA((2, 2, Part.sems)),
        pltpu.SemaphoreType.DMA((23,)),
        pltpu.SemaphoreType.DMA((23,)),
    ]
    held = pl.pallas_call(
        functools.partial(kernel, frames),
        out_shape=[pltpu.VMEM((frames, c), BF16)] * 2
        + [pltpu.VMEM(shape, BF16) for shape in fins]
        + [pltpu.VMEM((8, 128), F32)],
        in_specs=[any_spec, any_spec, any_spec, vmem, any_spec, vmem],
        out_specs=[vmem] * 7,
        scratch_shapes=scratch,
        compiler_params=pltpu.CompilerParams(
            collective_id=0, has_side_effects=True, vmem_limit_bytes=58 * 1024 * 1024
        ),
    )(
        inputs.reshape(frames, c),
        upstream.reshape(frames, c),
        first_layer_weight.reshape(3 * C, C),
        first_layer_bias,
        second_layer_weight.reshape(3 * C, C),
        second_layer_bias,
    )
    outs = pl.pallas_call(
        write_kernel,
        out_shape=[
            jax.ShapeDtypeStruct((frames, c), BF16),
            jax.ShapeDtypeStruct((frames, c), BF16),
            jax.ShapeDtypeStruct((3 * C, C), F32),
            jax.ShapeDtypeStruct((1, C), F32),
            jax.ShapeDtypeStruct((3 * C, C), F32),
            jax.ShapeDtypeStruct((1, C), F32),
        ],
        in_specs=[vmem] * 7,
        out_specs=[any_spec, any_spec, any_spec, vmem, any_spec, vmem],
        scratch_shapes=[
            pltpu.VMEM((3 * C, C), F32),
            pltpu.VMEM((3 * C, C), F32),
            pltpu.SemaphoreType.DMA((4,)),
        ],
        compiler_params=pltpu.CompilerParams(vmem_limit_bytes=8 * 1024 * 1024),
    )(*held)
    out, gin, gw1, gb1, gw2, gb2 = outs
    return (
        out.reshape(1, frames, c),
        gin.reshape(1, frames, c),
        gw1.reshape(3, C, C),
        gb1.reshape(C),
        gw2.reshape(3, C, C),
        gb2.reshape(C),
    )


def solution(mesh):
    return jax.shard_map(
        body,
        mesh=mesh,
        in_specs=(P("runs", "frames", None), P(), P(), P(), P(), P("runs", "frames", None)),
        out_specs=(P("runs", "frames", None), P("runs", "frames", None), P(), P(), P(), P()),
        check_vma=False,
    )
```

```python
import functools
import itertools
import math

import jax
import jax.numpy as jnp
from jax import lax
from jax.experimental import pallas as pl
from jax.experimental.pallas import tpu as pltpu
from jax.sharding import PartitionSpec as P

C = 256
D1 = 256
D2 = 512
HX = 1536
HH = 1024
R = 1024
F32 = jnp.float32
BF16 = jnp.bfloat16
C0 = math.sqrt(2.0 / math.pi)
C1 = C0 * 0.044715
MESH = pl.DeviceIdType.MESH


def gelu_parts(v):
    v2 = v * v
    t = jnp.tanh(v * (C0 + C1 * v2))
    h = 0.5 * v
    act = h + h * t
    slope = (0.5 + 0.5 * t) + (h * (1.0 - t * t)) * (C0 + (3.0 * C1) * v2)
    return act, slope


def dot(a, b):
    return jnp.dot(a, b, preferred_element_type=F32)


def dot_rows(a, b):
    return lax.dot_general(a, b, (((0,), (0,)), ((), ())), preferred_element_type=F32)


class Place:
    sizes = {"core": 2, "xy": 16, "z": 8}

    def __init__(self):
        self.f = lax.axis_index("frames")
        self.r = lax.axis_index("runs")
        self.core = lax.rem(self.f, 2)
        self.z = self.f // 4
        self.x = lax.rem(self.r, 2) * 2 + lax.rem(self.f // 2, 2)
        self.y = self.r // 2

    def device(self, core, x, y, z):
        return (z * 4 + lax.rem(x, 2) * 2 + core, y * 2 + x // 2)

    def index(self, group):
        return {"core": self.core, "xy": self.x * 4 + self.y, "z": self.z}[group]

    def others(self, group):
        if group == "core":
            o = 1 - self.core
            return [(o, self.device(o, self.x, self.y, self.z))]
        if group == "z":
            found = []
            for d in (4, 3, 5, 2, 6, 1, 7):
                o = lax.rem(self.z + d, 8)
                found.append((o, self.device(self.core, self.x, self.y, o)))
            return found
        steps = [s for s in itertools.product(range(4), range(4)) if any(s)]
        steps.sort(key=lambda s: -sum(min(v, 4 - v) for v in s))
        found = []
        for dx, dy in steps:
            x, y = lax.rem(self.x + dx, 4), lax.rem(self.y + dy, 4)
            found.append((x * 4 + y, self.device(self.core, x, y, self.z)))
        return found


class Sender:
    def __init__(self, place, send, recv):
        self.p, self.send, self.recv = place, send, recv
        self.sem = 0
        self.open = []
        self.sent = []

    def put(self, src, dst, to):
        copy = pltpu.make_async_remote_copy(
            src_ref=src,
            dst_ref=dst,
            send_sem=self.send.at[self.sem],
            recv_sem=self.recv.at[self.sem],
            device_id=to,
            device_id_type=MESH,
        )
        self.sem += 1
        copy.start()
        self.open.append(copy)
        self.sent.append(copy)

    def drain(self):
        for copy in self.open:
            copy.wait_recv()
        self.open = []

    def finish_sends(self):
        for copy in self.sent:
            copy.wait_send()


class Part(Sender):
    sems = 1 + 15 + 7 + 15 + 1

    def __init__(self, place, a, b, refs, send, recv):
        super().__init__(place, send, recv)
        self.a, self.b = a, b
        self.s0, self.r0, self.s1, self.r1, self.zb, self.fin = refs

    @staticmethod
    def shapes(a, b):
        n2 = Place.sizes[b]
        inner = (8, 2, 24, 128) if a == "xy" else (8, 24, 256)
        chunk = inner[-2:]
        n1 = Place.sizes[a]
        return [(2,) + inner, inner, inner, (n1 - 1,) + chunk, (n2,) + chunk], (2,) + inner

    def chunk(self, ref, lead, j):
        where = (j // 2, lax.rem(j, 2)) if self.a == "xy" else (j,)
        return ref.at[lead + where]

    def step0(self):
        for o, to in self.p.others("core"):
            self.put(self.s0.at[o], self.r0, to)

    def step1(self):
        self.drain()
        self.s1[...] = (self.s0[self.p.core].astype(F32) + self.r0[...].astype(F32)).astype(BF16)
        for d, (o, to) in enumerate(self.p.others(self.a)):
            self.put(self.chunk(self.s1, (), o), self.r1.at[d], to)

    def step2(self):
        self.drain()
        total = self.chunk(self.s1, (), self.p.index(self.a))[...].astype(F32)
        for d in range(Place.sizes[self.a] - 1):
            total = total + self.r1[d].astype(F32)
        i = self.p.index(self.b)
        self.zb[i] = total.astype(BF16)
        for o, to in self.p.others(self.b):
            self.put(self.zb.at[i], self.zb.at[i], to)

    def step3(self):
        self.drain()
        total = self.zb[0].astype(F32)
        for i in range(1, Place.sizes[self.b]):
            total = total + self.zb[i].astype(F32)
        mine = self.chunk(self.fin, (self.p.core,), self.p.index(self.a))
        mine[...] = total.astype(BF16)
        for o, to in self.p.others(self.a):
            self.put(mine, mine, to)

    def step4(self):
        self.drain()
        mine = self.fin.at[self.p.core]
        for o, to in self.p.others("core"):
            self.put(mine, mine, to)

    def pack(self, acc, row):
        if self.a == "xy":
            for h in range(2):
                piece = acc[pl.ds(row, 384), pl.ds(h * 128, 128)] * (1.0 / 1024.0)
                self.s0[:, :, h] = piece.reshape(2, 8, 24, 128).astype(BF16)
        else:
            piece = acc[pl.ds(row, 384), :] * (1.0 / 1024.0)
            self.s0[...] = piece.reshape(2, 8, 24, 256).astype(BF16)


class Layer:
    groups = (("xy", "z"), ("z", "xy"))

    def __init__(self, place, refs, fins, send, recv):
        self.parts = []
        for q, (a, b) in enumerate(self.groups):
            own = tuple(refs[q * 5 : q * 5 + 5]) + (fins[q],)
            self.parts.append(Part(place, a, b, own, send.at[q], recv.at[q]))

    def begin(self, acc):
        for q, part in enumerate(self.parts):
            part.pack(acc, q * 384)
            part.step0()

    def step(self, k):
        for part in self.parts:
            getattr(part, "step%d" % k)()

    def end(self):
        for part in self.parts:
            part.drain()

    def finish_sends(self):
        for part in self.parts:
            part.finish_sends()


class BiasSum(Sender):
    groups = ("core", "xy", "z")

    def __init__(self, place, slots, send, recv):
        super().__init__(place, send, recv)
        self.slots = slots

    def begin(self, level, value):
        group, buf = self.groups[level], self.slots[level]
        i = self.p.index(group)
        buf[i] = value
        for o, to in self.p.others(group):
            self.put(buf.at[i], buf.at[i], to)

    def finish(self, level):
        self.drain()
        buf = self.slots[level]
        total = buf[0]
        for i in range(1, Place.sizes[self.groups[level]]):
            total = total + buf[i]
        return total


def kernel(
    frames,
    x_hbm, up_hbm, w1_hbm, b1, w2_hbm, b2,
    outb, ginb, fin1a, fin1b, fin2a, fin2b, biases,
    xin, xc, up, hid, s1, g2, gh, g1, pout, pin, tout,
    w1, w2, w1t, w2t, acc1, acc2, db1, db2,
    *rest,
):
    nb = frames // R
    own = nb - 1
    bufs, rest = rest[:20], rest[20:]
    slots, rest = rest[:3], rest[3:]
    load_sem, halo_send, halo_recv, ar_send, ar_recv, bias_send, bias_recv = rest

    place = Place()
    f, r = place.f, place.r
    n = lax.axis_size("frames")
    after = (lax.rem(f + 1, n), r)
    before = (lax.rem(f + n - 1, n), r)

    barrier = pltpu.get_barrier_semaphore()
    peers = [after, before] + [to for g in Place.sizes for _, to in place.others(g)]
    for peer in peers:
        pl.semaphore_signal(barrier, inc=1, device_id=peer, device_id_type=MESH)

    tail = HX
    loads = [
        pltpu.make_async_copy(w1_hbm, w1, load_sem.at[0]),
        pltpu.make_async_copy(x_hbm.at[pl.ds(frames - tail, tail)], xin.at[pl.ds(HX + frames - tail, tail)], load_sem.at[1]),
        pltpu.make_async_copy(x_hbm.at[pl.ds(0, frames - tail)], xin.at[pl.ds(HX, frames - tail)], load_sem.at[2]),
        pltpu.make_async_copy(w2_hbm, w2, load_sem.at[3]),
        pltpu.make_async_copy(up_hbm, up, load_sem.at[4]),
        pltpu.make_async_copy(x_hbm.at[pl.ds(0, 2 * R)], xc.at[pl.ds(2 * D1, 2 * R)], load_sem.at[5]),
    ]
    for copy in loads:
        copy.start()

    def halo(k, src, dst, to):
        return pltpu.make_async_remote_copy(
            src_ref=src, dst_ref=dst, send_sem=halo_send.at[k], recv_sem=halo_recv.at[k],
            device_id=to, device_id_type=MESH,
        )

    send_x1 = halo(0, xin.at[pl.ds(HX + frames - 1024, 1024)], xin.at[pl.ds(HX - 1024, 1024)], after)
    send_x2 = halo(1, xin.at[pl.ds(HX + frames - HX, HX - 1024)], xin.at[pl.ds(0, HX - 1024)], after)
    send_p = halo(2, pout, pin, after)
    send_g1 = halo(3, g1.at[pl.ds(0, 2 * D1)], g1.at[pl.ds(HH + own * R, 2 * D1)], before)
    send_t = halo(4, tout, ginb.at[pl.ds(own * R, HH)], before)

    g2[pl.ds(0, HH), :] = jnp.zeros((HH, C), BF16)
    g2[pl.ds(HH + frames, HH), :] = jnp.zeros((HH, C), BF16)
    db1[...] = jnp.zeros_like(db1)
    db2[...] = jnp.zeros_like(db2)
    bias1 = b1[...].astype(F32).reshape(1, C)
    bias2 = b2[...].astype(F32).reshape(1, C)
    inner = jnp.where(f == 0, 0.0, 1.0).astype(F32)

    def rows(start, size=R):
        return pl.ds(start if isinstance(start, int) else pl.multiple_of(start, 256), size)

    def forward1(t, src, base, keep):
        x0 = src[rows(base + t), :]
        x1 = src[rows(base + t - D1), :]
        x2 = src[rows(base + t - 2 * D1), :]
        pre = dot(jnp.concatenate([x0, x1, x2], axis=1), w1[...]) + bias1
        act, slope = gelu_parts(pre)
        h = x0.astype(F32) + act
        hid[rows(t + HH), :] = (h if keep is None else h * keep).astype(BF16)
        s1[rows(t + HH), :] = slope

    def block_f1(b):
        forward1(b * R, xin, HX, None)

    def block_f2(b):
        t = b * R
        h = [hid[rows(t + HH - k * D2), :] for k in range(3)]
        pre = dot(jnp.concatenate(h, axis=1), w2[...]) + bias2
        act, slope = gelu_parts(pre)
        outb[rows(t), :] = (h[0].astype(F32) + act).astype(BF16)
        g = up[rows(t), :].astype(F32) * slope
        db2[...] += jnp.sum(g.reshape(R // 8, 8, C), axis=0)
        g2[rows(t + HH), :] = g.astype(BF16)

    def hidden_terms(t):
        cat = jnp.concatenate([g2[rows(t + HH + k * D2), :] for k in range(3)], axis=1)
        return dot(cat, w2t[...])

    def backward2(t, grad):
        gh[rows(t + HH), :] = grad
        g = grad * s1[rows(t + HH), :]
        db1[...] += jnp.sum(g.reshape(R // 8, 8, C), axis=0)
        g1[rows(t + HH), :] = g.astype(BF16)

    def block_b2(b):
        t = b * R
        backward2(t, hidden_terms(t) + up[rows(t), :].astype(F32))

    def block_p(b):
        t = b * R
        pout[rows(t - own * R), :] = (hidden_terms(t) + up[rows(t), :].astype(F32)).astype(BF16)

    def block_b1(b):
        t = b * R
        cat = jnp.concatenate([g1[rows(t + HH + k * D1), :] for k in range(3)], axis=1)
        ginb[rows(t), :] = (dot(cat, w1t[...]) + gh[rows(t + HH), :]).astype(BF16)

    def grad2(start, size, first=False):
        lhs = jnp.concatenate([hid[rows(start + HH - k * D2, size), :] for k in range(3)], axis=1)
        part = dot_rows(lhs, g2[rows(start + HH, size), :])
        acc2[...] = part if first else acc2[...] + part

    def grad1(start, size, first=False, src=None, base=HX):
        src = xin if src is None else src
        lhs = jnp.concatenate([src[rows(start + base - k * D1, size), :] for k in range(3)], axis=1)
        part = dot_rows(lhs, g1[rows(start + HH, size), :])
        acc1[...] = part if first else acc1[...] + part

    def loop(lo, hi, block):
        if hi - lo == 1:
            block(lo)
            return

        def body(b, _):
            block(b)
            return 0

        lax.fori_loop(lo, hi, body, 0)

    layer1 = Layer(place, bufs[:10], (fin1a, fin1b), ar_send.at[0], ar_recv.at[0])
    layer2 = Layer(place, bufs[10:], (fin2a, fin2b), ar_send.at[1], ar_recv.at[1])
    bias = BiasSum(place, slots, bias_send, bias_recv)

    loads[0].wait()
    loads[1].wait()
    block_f1(3)
    pl.semaphore_wait(barrier, len(peers))
    send_x1.start()
    send_x2.start()
    loads[2].wait()
    loop(1, 3, block_f1)
    loads[3].wait()
    loads[4].wait()
    for k in range(3):
        w2t[pl.ds(k * C, C), :] = w2[pl.ds(k * C, C), :].T
    block_f2(3)
    block_p(3)
    send_p.start()
    block_f2(2)
    block_b2(2)
    grad2(2 * R, 2 * R, True)
    grad1(2 * R, R, True)
    for k in range(3):
        w1t[pl.ds(k * C, C), :] = w1[pl.ds(k * C, C), :].T

    loads[5].wait()
    send_x1.wait_recv()
    xc[pl.ds(0, 2 * D1), :] = (xin[pl.ds(HX - 2 * D1, 2 * D1), :].astype(F32) * inner).astype(BF16)
    forward1(0, xc, 2 * D1, None)
    block_f2(1)
    send_x2.wait_recv()
    forward1(-R, xin, HX, inner)
    block_f2(0)
    loop(0, 2, block_b2)
    grad2(0, 2 * R)
    layer2.begin(acc2)
    grad1(0, 2 * R, False, xc, 2 * D1)
    layer2.step(1)
    send_p.wait_recv()
    backward2(-R, pin[...].astype(F32) + inner * hidden_terms(-R))
    send_g1.start()
    grad1(-R, R)
    layer1.begin(acc1)
    both = jnp.concatenate(
        [jnp.sum(v[...], axis=0, keepdims=True)[:, h * 128 : (h + 1) * 128] for v in (db2, db1) for h in range(2)]
        + [jnp.zeros((4, 128), F32)],
        axis=0,
    ) * (1.0 / 1024.0)
    bias.begin(0, both)

    edge = (g1[pl.ds(HH, 2 * D1), :].astype(F32) * inner).astype(BF16)
    cat = jnp.concatenate(
        [
            g1[pl.ds(0, R), :],
            jnp.concatenate([g1[pl.ds(D1, R - D1), :], edge[:D1]], axis=0),
            jnp.concatenate([g1[pl.ds(2 * D1, R - 2 * D1), :], edge], axis=0),
        ],
        axis=1,
    )
    tout[...] = (dot(cat, w1t[...]) + gh[pl.ds(0, R), :]).astype(BF16)
    send_t.start()
    layer1.step(1)
    bias.begin(1, bias.finish(0))
    loop(0, own - 1, block_b1)
    layer2.step(2)
    send_g1.wait_recv()
    loop(own - 1, own, block_b1)
    layer1.step(2)
    bias.begin(2, bias.finish(1))
    layer2.step(3)
    layer1.step(3)
    biases[...] = bias.finish(2)
    layer2.step(4)
    layer1.step(4)
    layer2.end()
    send_t.wait_recv()
    for copy in (send_x1, send_x2, send_p, send_g1, send_t):
        copy.wait_send()
    bias.finish_sends()
    layer2.finish_sends()
    layer1.finish_sends()
    layer1.end()


def write_kernel(outb, ginb, fin1a, fin1b, fin2a, fin2b, biases, out, gin, gw1, gb1, gw2, gb2, wide1, wide2, sem):
    copies = [pltpu.make_async_copy(outb, out, sem.at[0]), pltpu.make_async_copy(ginb, gin, sem.at[1])]
    for copy in copies:
        copy.start()
    for k, (a, b, wide, dst) in enumerate(((fin1a, fin1b, wide1, gw1), (fin2a, fin2b, wide2, gw2))):
        for h in range(2):
            wide[pl.ds(0, 384), pl.ds(h * 128, 128)] = a[:, :, h].astype(F32).reshape(384, 128)
        wide[pl.ds(384, 384), :] = b[...].astype(F32).reshape(384, 256)
        copies.append(pltpu.make_async_copy(wide, dst, sem.at[2 + k]))
        copies[-1].start()
    for h in range(2):
        gb2[:, pl.ds(h * 128, 128)] = biases[pl.ds(h, 1), :]
        gb1[:, pl.ds(h * 128, 128)] = biases[pl.ds(2 + h, 1), :]
    for copy in copies:
        copy.wait()


def body(inputs, first_layer_weight, first_layer_bias, second_layer_weight, second_layer_bias, upstream):
    _, frames, c = inputs.shape
    any_spec = pl.BlockSpec(memory_space=pl.ANY)
    vmem = pl.BlockSpec(memory_space=pltpu.VMEM)
    nb = frames // R
    scratch = [
        pltpu.VMEM((HX + frames, C), BF16),
        pltpu.VMEM((2 * R + 2 * D1, C), BF16),
        pltpu.VMEM((frames, C), BF16),
        pltpu.VMEM((HH + frames, C), BF16),
        pltpu.VMEM((HH + frames, C), F32),
        pltpu.VMEM((HH + frames + HH, C), BF16),
        pltpu.VMEM((frames, C), F32),
        pltpu.VMEM((frames + 2 * D1, C), BF16),
        pltpu.VMEM((HH, C), BF16),
        pltpu.VMEM((HH, C), BF16),
        pltpu.VMEM((HH, C), BF16),
        pltpu.VMEM((3 * C, C), BF16),
        pltpu.VMEM((3 * C, C), BF16),
        pltpu.VMEM((3 * C, C), BF16),
        pltpu.VMEM((3 * C, C), BF16),
        pltpu.VMEM((3 * C, C), F32),
        pltpu.VMEM((3 * C, C), F32),
        pltpu.VMEM((8, C), F32),
        pltpu.VMEM((8, C), F32),
    ]
    scratch += [pltpu.VMEM(s, BF16) for _ in range(2) for a, b in Layer.groups for s in Part.shapes(a, b)[0]]
    fins = [Part.shapes(a, b)[1] for _ in range(2) for a, b in Layer.groups]
    scratch += [pltpu.VMEM((k, 8, 128), F32) for k in (2, 16, 8)]
    scratch += [
        pltpu.SemaphoreType.DMA((6,)),
        pltpu.SemaphoreType.DMA((5,)),
        pltpu.SemaphoreType.DMA((5,)),
        pltpu.SemaphoreType.DMA((2, 2, Part.sems)),
        pltpu.SemaphoreType.DMA((2, 2, Part.sems)),
        pltpu.SemaphoreType.DMA((23,)),
        pltpu.SemaphoreType.DMA((23,)),
    ]
    held = pl.pallas_call(
        functools.partial(kernel, frames),
        out_shape=[pltpu.VMEM((frames, c), BF16)] * 2
        + [pltpu.VMEM(shape, BF16) for shape in fins]
        + [pltpu.VMEM((8, 128), F32)],
        in_specs=[any_spec, any_spec, any_spec, vmem, any_spec, vmem],
        out_specs=[vmem] * 7,
        scratch_shapes=scratch,
        compiler_params=pltpu.CompilerParams(
            collective_id=0, has_side_effects=True, vmem_limit_bytes=58 * 1024 * 1024
        ),
    )(
        inputs.reshape(frames, c),
        upstream.reshape(frames, c),
        first_layer_weight.reshape(3 * C, C),
        first_layer_bias,
        second_layer_weight.reshape(3 * C, C),
        second_layer_bias,
    )
    outs = pl.pallas_call(
        write_kernel,
        out_shape=[
            jax.ShapeDtypeStruct((frames, c), BF16),
            jax.ShapeDtypeStruct((frames, c), BF16),
            jax.ShapeDtypeStruct((3 * C, C), F32),
            jax.ShapeDtypeStruct((1, C), F32),
            jax.ShapeDtypeStruct((3 * C, C), F32),
            jax.ShapeDtypeStruct((1, C), F32),
        ],
        in_specs=[vmem] * 7,
        out_specs=[any_spec, any_spec, any_spec, vmem, any_spec, vmem],
        scratch_shapes=[
            pltpu.VMEM((3 * C, C), F32),
            pltpu.VMEM((3 * C, C), F32),
            pltpu.SemaphoreType.DMA((4,)),
        ],
        compiler_params=pltpu.CompilerParams(vmem_limit_bytes=8 * 1024 * 1024),
    )(*held)
    out, gin, gw1, gb1, gw2, gb2 = outs
    return (
        out.reshape(1, frames, c),
        gin.reshape(1, frames, c),
        gw1.reshape(3, C, C),
        gb1.reshape(C),
        gw2.reshape(3, C, C),
        gb2.reshape(C),
    )


def solution(mesh):
    return jax.shard_map(
        body,
        mesh=mesh,
        in_specs=(P("runs", "frames", None), P(), P(), P(), P(), P("runs", "frames", None)),
        out_specs=(P("runs", "frames", None), P("runs", "frames", None), P(), P(), P(), P()),
        check_vma=False,
    )
```

```python
import functools
import itertools
import math

import jax
import jax.numpy as jnp
from jax import lax
from jax.experimental import pallas as pl
from jax.experimental.pallas import tpu as pltpu
from jax.sharding import PartitionSpec as P

C = 256
D1 = 256
D2 = 512
HX = 1536
HH = 1024
R = 1024
F32 = jnp.float32
BF16 = jnp.bfloat16
C0 = math.sqrt(2.0 / math.pi)
C1 = C0 * 0.044715
MESH = pl.DeviceIdType.MESH


def gelu_parts(v):
    v2 = v * v
    t = jnp.tanh(v * (C0 + C1 * v2))
    h = 0.5 * v
    act = h + h * t
    slope = (0.5 + 0.5 * t) + (h * (1.0 - t * t)) * (C0 + (3.0 * C1) * v2)
    return act, slope


def dot(a, b):
    return jnp.dot(a, b, preferred_element_type=F32)


def dot_rows(a, b):
    return lax.dot_general(a, b, (((0,), (0,)), ((), ())), preferred_element_type=F32)


class Place:
    sizes = {"core": 2, "xy": 16, "z": 8}

    def __init__(self):
        self.f = lax.axis_index("frames")
        self.r = lax.axis_index("runs")
        self.core = lax.rem(self.f, 2)
        self.z = self.f // 4
        self.x = lax.rem(self.r, 2) * 2 + lax.rem(self.f // 2, 2)
        self.y = self.r // 2

    def device(self, core, x, y, z):
        return (z * 4 + lax.rem(x, 2) * 2 + core, y * 2 + x // 2)

    def index(self, group):
        return {"core": self.core, "xy": self.x * 4 + self.y, "z": self.z}[group]

    def others(self, group):
        if group == "core":
            o = 1 - self.core
            return [(o, self.device(o, self.x, self.y, self.z))]
        if group == "z":
            found = []
            for d in (4, 3, 5, 2, 6, 1, 7):
                o = lax.rem(self.z + d, 8)
                found.append((o, self.device(self.core, self.x, self.y, o)))
            return found
        steps = [s for s in itertools.product(range(4), range(4)) if any(s)]
        steps.sort(key=lambda s: -sum(min(v, 4 - v) for v in s))
        found = []
        for dx, dy in steps:
            x, y = lax.rem(self.x + dx, 4), lax.rem(self.y + dy, 4)
            found.append((x * 4 + y, self.device(self.core, x, y, self.z)))
        return found


class Sender:
    def __init__(self, place, send, recv):
        self.p, self.send, self.recv = place, send, recv
        self.sem = 0
        self.open = []
        self.sent = []

    def put(self, src, dst, to):
        copy = pltpu.make_async_remote_copy(
            src_ref=src,
            dst_ref=dst,
            send_sem=self.send.at[self.sem],
            recv_sem=self.recv.at[self.sem],
            device_id=to,
            device_id_type=MESH,
        )
        self.sem += 1
        copy.start()
        self.open.append(copy)
        self.sent.append(copy)

    def drain(self):
        for copy in self.open:
            copy.wait_recv()
        self.open = []

    def finish_sends(self):
        for copy in self.sent:
            copy.wait_send()


class Part(Sender):
    sems = 1 + 15 + 7 + 15 + 1

    def __init__(self, place, a, b, refs, send, recv):
        super().__init__(place, send, recv)
        self.a, self.b = a, b
        self.s0, self.r0, self.s1, self.r1, self.zb, self.fin = refs

    @staticmethod
    def shapes(a, b):
        n2 = Place.sizes[b]
        inner = (8, 2, 24, 128) if a == "xy" else (8, 24, 256)
        chunk = inner[-2:]
        n1 = Place.sizes[a]
        return [(2,) + inner, inner, inner, (n1 - 1,) + chunk, (n2,) + chunk], (2,) + inner

    def chunk(self, ref, lead, j):
        where = (j // 2, lax.rem(j, 2)) if self.a == "xy" else (j,)
        return ref.at[lead + where]

    def step0(self):
        for o, to in self.p.others("core"):
            self.put(self.s0.at[o], self.r0, to)

    def step1(self):
        self.drain()
        self.s1[...] = (self.s0[self.p.core].astype(F32) + self.r0[...].astype(F32)).astype(BF16)
        for d, (o, to) in enumerate(self.p.others(self.a)):
            self.put(self.chunk(self.s1, (), o), self.r1.at[d], to)

    def step2(self):
        self.drain()
        total = self.chunk(self.s1, (), self.p.index(self.a))[...].astype(F32)
        for d in range(Place.sizes[self.a] - 1):
            total = total + self.r1[d].astype(F32)
        i = self.p.index(self.b)
        self.zb[i] = total.astype(BF16)
        for o, to in self.p.others(self.b):
            self.put(self.zb.at[i], self.zb.at[i], to)

    def step3(self):
        self.drain()
        total = self.zb[0].astype(F32)
        for i in range(1, Place.sizes[self.b]):
            total = total + self.zb[i].astype(F32)
        mine = self.chunk(self.fin, (self.p.core,), self.p.index(self.a))
        mine[...] = total.astype(BF16)
        for o, to in self.p.others(self.a):
            self.put(mine, mine, to)

    def step4(self):
        self.drain()
        mine = self.fin.at[self.p.core]
        for o, to in self.p.others("core"):
            self.put(mine, mine, to)

    def pack(self, acc, row):
        if self.a == "xy":
            for h in range(2):
                piece = acc[pl.ds(row, 384), pl.ds(h * 128, 128)] * (1.0 / 1024.0)
                self.s0[:, :, h] = piece.reshape(2, 8, 24, 128).astype(BF16)
        else:
            piece = acc[pl.ds(row, 384), :] * (1.0 / 1024.0)
            self.s0[...] = piece.reshape(2, 8, 24, 256).astype(BF16)


class Layer:
    groups = (("xy", "z"), ("z", "xy"))

    def __init__(self, place, refs, fins, send, recv):
        self.parts = []
        for q, (a, b) in enumerate(self.groups):
            own = tuple(refs[q * 5 : q * 5 + 5]) + (fins[q],)
            self.parts.append(Part(place, a, b, own, send.at[q], recv.at[q]))

    def begin(self, acc):
        for q, part in enumerate(self.parts):
            part.pack(acc, q * 384)
            part.step0()

    def step(self, k):
        for part in self.parts:
            getattr(part, "step%d" % k)()

    def end(self):
        for part in self.parts:
            part.drain()

    def finish_sends(self):
        for part in self.parts:
            part.finish_sends()


class BiasSum(Sender):
    groups = ("core", "xy", "z")

    def __init__(self, place, slots, send, recv):
        super().__init__(place, send, recv)
        self.slots = slots

    def begin(self, level, value):
        group, buf = self.groups[level], self.slots[level]
        i = self.p.index(group)
        buf[i] = value
        for o, to in self.p.others(group):
            self.put(buf.at[i], buf.at[i], to)

    def finish(self, level):
        self.drain()
        buf = self.slots[level]
        total = buf[0]
        for i in range(1, Place.sizes[self.groups[level]]):
            total = total + buf[i]
        return total


def kernel(
    frames,
    x_hbm, up_hbm, w1_hbm, b1, w2_hbm, b2,
    outb, ginb, fin1a, fin1b, fin2a, fin2b, biases,
    xin, xc, up, hid, s1, g2, g2h, gh, g1, pout, pin,
    w1, w2, w1t, w2t, acc1, acc2, db1, db2,
    *rest,
):
    nb = frames // R
    own = nb - 1
    bufs, rest = rest[:20], rest[20:]
    slots, rest = rest[:3], rest[3:]
    load_sem, halo_send, halo_recv, ar_send, ar_recv, bias_send, bias_recv = rest

    place = Place()
    f, r = place.f, place.r
    n = lax.axis_size("frames")
    after = (lax.rem(f + 1, n), r)
    before = (lax.rem(f + n - 1, n), r)

    barrier = pltpu.get_barrier_semaphore()
    peers = [after, before] + [to for g in Place.sizes for _, to in place.others(g)]
    for peer in peers:
        pl.semaphore_signal(barrier, inc=1, device_id=peer, device_id_type=MESH)

    tail = HX
    loads = [
        pltpu.make_async_copy(w1_hbm, w1, load_sem.at[0]),
        pltpu.make_async_copy(x_hbm.at[pl.ds(frames - tail, tail)], xin.at[pl.ds(HX + frames - tail, tail)], load_sem.at[1]),
        pltpu.make_async_copy(x_hbm.at[pl.ds(0, frames - tail)], xin.at[pl.ds(HX, frames - tail)], load_sem.at[2]),
        pltpu.make_async_copy(w2_hbm, w2, load_sem.at[3]),
        pltpu.make_async_copy(up_hbm, up, load_sem.at[4]),
        pltpu.make_async_copy(x_hbm.at[pl.ds(0, 2 * R)], xc.at[pl.ds(2 * D1, 2 * R)], load_sem.at[5]),
    ]
    for copy in loads:
        copy.start()

    def halo(k, src, dst, to):
        return pltpu.make_async_remote_copy(
            src_ref=src, dst_ref=dst, send_sem=halo_send.at[k], recv_sem=halo_recv.at[k],
            device_id=to, device_id_type=MESH,
        )

    send_x1 = halo(0, xin.at[pl.ds(HX + frames - 1024, 1024)], xin.at[pl.ds(HX - 1024, 1024)], after)
    send_x2 = halo(1, xin.at[pl.ds(HX + frames - HX, HX - 1024)], xin.at[pl.ds(0, HX - 1024)], after)
    send_p = halo(2, pout, pin, after)
    send_g2 = [halo(3 + i, g2.at[pl.ds(HH + i * D1, D1)], g2h.at[pl.ds(i * D1, D1)], before) for i in range(4)]
    send_g1 = [
        halo(7 + i, g1.at[pl.ds(HH + i * D1, D1)], g1.at[pl.ds(HH + frames + i * D1, D1)], before) for i in range(2)
    ]

    g2[pl.ds(0, HH), :] = jnp.zeros((HH, C), BF16)
    g2[pl.ds(HH + frames, HH), :] = jnp.zeros((HH, C), BF16)
    db1[...] = jnp.zeros_like(db1)
    db2[...] = jnp.zeros_like(db2)
    bias1 = b1[...].astype(F32).reshape(1, C)
    bias2 = b2[...].astype(F32).reshape(1, C)
    inner = jnp.where(f == 0, 0.0, 1.0).astype(F32)
    outer = jnp.where(f == n - 1, 0.0, 1.0).astype(F32)

    def rows(start, size=R):
        return pl.ds(start if isinstance(start, int) else pl.multiple_of(start, 256), size)

    def forward1(t, src, base, keep):
        x0 = src[rows(base + t), :]
        x1 = src[rows(base + t - D1), :]
        x2 = src[rows(base + t - 2 * D1), :]
        pre = dot(jnp.concatenate([x0, x1, x2], axis=1), w1[...]) + bias1
        act, slope = gelu_parts(pre)
        h = x0.astype(F32) + act
        hid[rows(t + HH), :] = (h if keep is None else h * keep).astype(BF16)
        s1[rows(t + HH), :] = slope

    def block_f1(b):
        forward1(b * R, xin, HX, None)

    def block_f2(b):
        t = b * R
        h = [hid[rows(t + HH - k * D2), :] for k in range(3)]
        pre = dot(jnp.concatenate(h, axis=1), w2[...]) + bias2
        act, slope = gelu_parts(pre)
        outb[rows(t), :] = (h[0].astype(F32) + act).astype(BF16)
        g = up[rows(t), :].astype(F32) * slope
        db2[...] += jnp.sum(g.reshape(R // 8, 8, C), axis=0)
        g2[rows(t + HH), :] = g.astype(BF16)

    def hidden_terms(t):
        cat = jnp.concatenate([g2[rows(t + HH + k * D2), :] for k in range(3)], axis=1)
        return dot(cat, w2t[...])

    def backward2(t, grad, summed=True):
        if not (isinstance(t, int) and t < 0):
            gh[rows(t), :] = grad
        g = grad * s1[rows(t + HH), :]
        if summed:
            db1[...] += jnp.sum(g.reshape(R // 8, 8, C), axis=0)
        g1[rows(t + HH), :] = g.astype(BF16)

    def block_b2_last():
        t = frames - R
        near, far = g2[rows(t + HH), :], g2h[...]
        mixed = jnp.concatenate([g2[rows(t + HH + D2, R - D2), :], far[:D2]], axis=0)
        terms = dot(jnp.concatenate([near, mixed, far], axis=1), w2t[...])
        backward2(t, terms + up[rows(t), :].astype(F32), False)

    def block_b2(b):
        t = b * R
        backward2(t, hidden_terms(t) + up[rows(t), :].astype(F32))

    def block_p(b):
        t = b * R
        pout[rows(t - own * R), :] = (hidden_terms(t) + up[rows(t), :].astype(F32)).astype(BF16)

    def block_b1(b):
        t = b * R
        cat = jnp.concatenate([g1[rows(t + HH + k * D1), :] for k in range(3)], axis=1)
        ginb[rows(t), :] = (dot(cat, w1t[...]) + gh[rows(t), :]).astype(BF16)

    def grad2(start, size, first=False):
        lhs = jnp.concatenate([hid[rows(start + HH - k * D2, size), :] for k in range(3)], axis=1)
        part = dot_rows(lhs, g2[rows(start + HH, size), :])
        acc2[...] = part if first else acc2[...] + part

    def grad1(start, size, first=False, src=None, base=HX):
        src = xin if src is None else src
        lhs = jnp.concatenate([src[rows(start + base - k * D1, size), :] for k in range(3)], axis=1)
        part = dot_rows(lhs, g1[rows(start + HH, size), :])
        acc1[...] = part if first else acc1[...] + part

    def loop(lo, hi, block):
        if hi - lo == 1:
            block(lo)
            return

        def body(b, _):
            block(b)
            return 0

        lax.fori_loop(lo, hi, body, 0)

    layer1 = Layer(place, bufs[:10], (fin1a, fin1b), ar_send.at[0], ar_recv.at[0])
    layer2 = Layer(place, bufs[10:], (fin2a, fin2b), ar_send.at[1], ar_recv.at[1])
    bias = BiasSum(place, slots, bias_send, bias_recv)

    loads[0].wait()
    loads[1].wait()
    block_f1(3)
    pl.semaphore_wait(barrier, len(peers))
    send_x1.start()
    send_x2.start()
    loads[2].wait()
    loop(1, 3, block_f1)
    loads[3].wait()
    loads[4].wait()
    for k in range(3):
        w2t[pl.ds(k * C, C), :] = w2[pl.ds(k * C, C), :].T
    block_f2(3)
    block_p(3)
    send_p.start()
    block_f2(2)
    block_b2(2)
    grad2(2 * R, 2 * R, True)
    grad1(2 * R, R, True)
    for k in range(3):
        w1t[pl.ds(k * C, C), :] = w1[pl.ds(k * C, C), :].T

    loads[5].wait()
    send_x1.wait_recv()
    xc[pl.ds(0, 2 * D1), :] = (xin[pl.ds(HX - 2 * D1, 2 * D1), :].astype(F32) * inner).astype(BF16)
    forward1(0, xc, 2 * D1, None)
    block_f2(1)
    send_x2.wait_recv()
    forward1(-R, xin, HX, inner)
    block_f2(0)
    send_g2[0].start()
    send_g2[1].start()
    block_b2(1)
    block_b2(0)
    send_g2[2].start()
    grad2(0, 2 * R)
    layer2.begin(acc2)
    send_g2[3].start()
    grad1(0, 2 * R, False, xc, 2 * D1)
    layer2.step(1)
    send_g1[0].start()
    send_p.wait_recv()
    backward2(-R, pin[...].astype(F32) + inner * hidden_terms(-R))
    grad1(-R, R)
    layer1.begin(acc1)
    both = jnp.concatenate(
        [jnp.sum(v[...], axis=0, keepdims=True)[:, h * 128 : (h + 1) * 128] for v in (db2, db1) for h in range(2)]
        + [jnp.zeros((4, 128), F32)],
        axis=0,
    ) * (1.0 / 1024.0)
    bias.begin(0, both)
    send_g1[1].start()
    loop(0, 2, block_b1)
    layer1.step(1)
    bias.begin(1, bias.finish(0))
    for copy in send_g2:
        copy.wait_recv()
    g2h[...] = (g2h[...].astype(F32) * outer).astype(BF16)
    block_b2_last()
    block_b1(2)
    layer2.step(2)
    for copy in send_g1:
        copy.wait_recv()
    edge = pl.ds(HH + frames, 2 * D1)
    g1[edge, :] = (g1[edge, :].astype(F32) * outer).astype(BF16)
    block_b1(3)
    layer1.step(2)
    bias.begin(2, bias.finish(1))
    layer2.step(3)
    layer1.step(3)
    biases[...] = bias.finish(2)
    layer2.step(4)
    layer1.step(4)
    layer2.end()
    for copy in [send_x1, send_x2, send_p] + send_g2 + send_g1:
        copy.wait_send()
    bias.finish_sends()
    layer2.finish_sends()
    layer1.finish_sends()
    layer1.end()


def write_kernel(outb, ginb, fin1a, fin1b, fin2a, fin2b, biases, out, gin, gw1, gb1, gw2, gb2, wide1, wide2, sem):
    copies = [pltpu.make_async_copy(outb, out, sem.at[0]), pltpu.make_async_copy(ginb, gin, sem.at[1])]
    for copy in copies:
        copy.start()
    for k, (a, b, wide, dst) in enumerate(((fin1a, fin1b, wide1, gw1), (fin2a, fin2b, wide2, gw2))):
        for h in range(2):
            wide[pl.ds(0, 384), pl.ds(h * 128, 128)] = a[:, :, h].astype(F32).reshape(384, 128)
        wide[pl.ds(384, 384), :] = b[...].astype(F32).reshape(384, 256)
        copies.append(pltpu.make_async_copy(wide, dst, sem.at[2 + k]))
        copies[-1].start()
    for h in range(2):
        gb2[:, pl.ds(h * 128, 128)] = biases[pl.ds(h, 1), :]
        gb1[:, pl.ds(h * 128, 128)] = biases[pl.ds(2 + h, 1), :]
    for copy in copies:
        copy.wait()


def body(inputs, first_layer_weight, first_layer_bias, second_layer_weight, second_layer_bias, upstream):
    _, frames, c = inputs.shape
    any_spec = pl.BlockSpec(memory_space=pl.ANY)
    vmem = pl.BlockSpec(memory_space=pltpu.VMEM)
    nb = frames // R
    scratch = [
        pltpu.VMEM((HX + frames, C), BF16),
        pltpu.VMEM((2 * R + 2 * D1, C), BF16),
        pltpu.VMEM((frames, C), BF16),
        pltpu.VMEM((HH + frames, C), BF16),
        pltpu.VMEM((HH + frames, C), F32),
        pltpu.VMEM((HH + frames + HH, C), BF16),
        pltpu.VMEM((HH, C), BF16),
        pltpu.VMEM((frames, C), F32),
        pltpu.VMEM((HH + frames + 2 * D1, C), BF16),
        pltpu.VMEM((HH, C), BF16),
        pltpu.VMEM((HH, C), BF16),
        pltpu.VMEM((3 * C, C), BF16),
        pltpu.VMEM((3 * C, C), BF16),
        pltpu.VMEM((3 * C, C), BF16),
        pltpu.VMEM((3 * C, C), BF16),
        pltpu.VMEM((3 * C, C), F32),
        pltpu.VMEM((3 * C, C), F32),
        pltpu.VMEM((8, C), F32),
        pltpu.VMEM((8, C), F32),
    ]
    scratch += [pltpu.VMEM(s, BF16) for _ in range(2) for a, b in Layer.groups for s in Part.shapes(a, b)[0]]
    fins = [Part.shapes(a, b)[1] for _ in range(2) for a, b in Layer.groups]
    scratch += [pltpu.VMEM((k, 8, 128), F32) for k in (2, 16, 8)]
    scratch += [
        pltpu.SemaphoreType.DMA((6,)),
        pltpu.SemaphoreType.DMA((9,)),
        pltpu.SemaphoreType.DMA((9,)),
        pltpu.SemaphoreType.DMA((2, 2, Part.sems)),
        pltpu.SemaphoreType.DMA((2, 2, Part.sems)),
        pltpu.SemaphoreType.DMA((23,)),
        pltpu.SemaphoreType.DMA((23,)),
    ]
    held = pl.pallas_call(
        functools.partial(kernel, frames),
        out_shape=[pltpu.VMEM((frames, c), BF16)] * 2
        + [pltpu.VMEM(shape, BF16) for shape in fins]
        + [pltpu.VMEM((8, 128), F32)],
        in_specs=[any_spec, any_spec, any_spec, vmem, any_spec, vmem],
        out_specs=[vmem] * 7,
        scratch_shapes=scratch,
        compiler_params=pltpu.CompilerParams(
            collective_id=0, has_side_effects=True, vmem_limit_bytes=58 * 1024 * 1024
        ),
    )(
        inputs.reshape(frames, c),
        upstream.reshape(frames, c),
        first_layer_weight.reshape(3 * C, C),
        first_layer_bias,
        second_layer_weight.reshape(3 * C, C),
        second_layer_bias,
    )
    outs = pl.pallas_call(
        write_kernel,
        out_shape=[
            jax.ShapeDtypeStruct((frames, c), BF16),
            jax.ShapeDtypeStruct((frames, c), BF16),
            jax.ShapeDtypeStruct((3 * C, C), F32),
            jax.ShapeDtypeStruct((1, C), F32),
            jax.ShapeDtypeStruct((3 * C, C), F32),
            jax.ShapeDtypeStruct((1, C), F32),
        ],
        in_specs=[vmem] * 7,
        out_specs=[any_spec, any_spec, any_spec, vmem, any_spec, vmem],
        scratch_shapes=[
            pltpu.VMEM((3 * C, C), F32),
            pltpu.VMEM((3 * C, C), F32),
            pltpu.SemaphoreType.DMA((4,)),
        ],
        compiler_params=pltpu.CompilerParams(vmem_limit_bytes=8 * 1024 * 1024),
    )(*held)
    out, gin, gw1, gb1, gw2, gb2 = outs
    return (
        out.reshape(1, frames, c),
        gin.reshape(1, frames, c),
        gw1.reshape(3, C, C),
        gb1.reshape(C),
        gw2.reshape(3, C, C),
        gb2.reshape(C),
    )


def solution(mesh):
    return jax.shard_map(
        body,
        mesh=mesh,
        in_specs=(P("runs", "frames", None), P(), P(), P(), P(), P("runs", "frames", None)),
        out_specs=(P("runs", "frames", None), P("runs", "frames", None), P(), P(), P(), P()),
        check_vma=False,
    )
```

```python
import functools
import itertools
import math

import jax
import jax.numpy as jnp
from jax import lax
from jax.experimental import pallas as pl
from jax.experimental.pallas import tpu as pltpu
from jax.sharding import PartitionSpec as P

C = 256
D1 = 256
D2 = 512
HX = 1536
HH = 1024
R = 1024
F32 = jnp.float32
BF16 = jnp.bfloat16
C0 = math.sqrt(2.0 / math.pi)
C1 = C0 * 0.044715
MESH = pl.DeviceIdType.MESH


def gelu_parts(v):
    v2 = v * v
    t = jnp.tanh(v * (C0 + C1 * v2))
    s = 0.5 + 0.5 * t
    slope = s + (s - s * t) * (v * (C0 + (3.0 * C1) * v2))
    return v * s, slope


def dot(a, b):
    return jnp.dot(a, b, preferred_element_type=F32)


def dot_rows(a, b):
    return lax.dot_general(a, b, (((0,), (0,)), ((), ())), preferred_element_type=F32)


class Place:
    sizes = {"core": 2, "xy": 16, "z": 8}

    def __init__(self):
        self.f = lax.axis_index("frames")
        self.r = lax.axis_index("runs")
        self.core = lax.rem(self.f, 2)
        self.z = self.f // 4
        self.x = lax.rem(self.r, 2) * 2 + lax.rem(self.f // 2, 2)
        self.y = self.r // 2

    def device(self, core, x, y, z):
        return (z * 4 + lax.rem(x, 2) * 2 + core, y * 2 + x // 2)

    def index(self, group):
        return {"core": self.core, "xy": self.x * 4 + self.y, "z": self.z}[group]

    def others(self, group):
        if group == "core":
            o = 1 - self.core
            return [(o, self.device(o, self.x, self.y, self.z))]
        if group == "z":
            found = []
            for d in (4, 3, 5, 2, 6, 1, 7):
                o = lax.rem(self.z + d, 8)
                found.append((o, self.device(self.core, self.x, self.y, o)))
            return found
        steps = [s for s in itertools.product(range(4), range(4)) if any(s)]
        steps.sort(key=lambda s: -sum(min(v, 4 - v) for v in s))
        found = []
        for dx, dy in steps:
            x, y = lax.rem(self.x + dx, 4), lax.rem(self.y + dy, 4)
            found.append((x * 4 + y, self.device(self.core, x, y, self.z)))
        return found


class Sender:
    def __init__(self, place, send, recv):
        self.p, self.send, self.recv = place, send, recv
        self.sem = 0
        self.open = []
        self.sent = []

    def put(self, src, dst, to):
        copy = pltpu.make_async_remote_copy(
            src_ref=src,
            dst_ref=dst,
            send_sem=self.send.at[self.sem],
            recv_sem=self.recv.at[self.sem],
            device_id=to,
            device_id_type=MESH,
        )
        self.sem += 1
        copy.start()
        self.open.append(copy)
        self.sent.append(copy)

    def drain(self):
        for copy in self.open:
            copy.wait_recv()
        self.open = []

    def finish_sends(self):
        for copy in self.sent:
            copy.wait_send()


class Part(Sender):
    sems = 1 + 15 + 7 + 15 + 1

    def __init__(self, place, a, b, refs, send, recv):
        super().__init__(place, send, recv)
        self.a, self.b = a, b
        self.s0, self.r0, self.s1, self.r1, self.zb, self.fin = refs

    @staticmethod
    def shapes(a, b):
        n2 = Place.sizes[b]
        inner = (8, 2, 24, 128) if a == "xy" else (8, 24, 256)
        chunk = inner[-2:]
        n1 = Place.sizes[a]
        return [(2,) + inner, inner, inner, (n1 - 1,) + chunk, (n2,) + chunk], (2,) + inner

    def chunk(self, ref, lead, j):
        where = (j // 2, lax.rem(j, 2)) if self.a == "xy" else (j,)
        return ref.at[lead + where]

    def step0(self):
        for o, to in self.p.others("core"):
            self.put(self.s0.at[o], self.r0, to)

    def step1(self):
        self.drain()
        self.s1[...] = (self.s0[self.p.core].astype(F32) + self.r0[...].astype(F32)).astype(BF16)
        for d, (o, to) in enumerate(self.p.others(self.a)):
            self.put(self.chunk(self.s1, (), o), self.r1.at[d], to)

    def step2(self):
        self.drain()
        total = self.chunk(self.s1, (), self.p.index(self.a))[...].astype(F32)
        for d in range(Place.sizes[self.a] - 1):
            total = total + self.r1[d].astype(F32)
        i = self.p.index(self.b)
        self.zb[i] = total.astype(BF16)
        for o, to in self.p.others(self.b):
            self.put(self.zb.at[i], self.zb.at[i], to)

    def step3(self):
        self.drain()
        total = self.zb[0].astype(F32)
        for i in range(1, Place.sizes[self.b]):
            total = total + self.zb[i].astype(F32)
        mine = self.chunk(self.fin, (self.p.core,), self.p.index(self.a))
        mine[...] = total.astype(BF16)
        for o, to in self.p.others(self.a):
            self.put(mine, mine, to)

    def step4(self):
        self.drain()
        mine = self.fin.at[self.p.core]
        for o, to in self.p.others("core"):
            self.put(mine, mine, to)

    def pack(self, acc, row):
        if self.a == "xy":
            for h in range(2):
                piece = acc[pl.ds(row, 384), pl.ds(h * 128, 128)] * (1.0 / 1024.0)
                self.s0[:, :, h] = piece.reshape(2, 8, 24, 128).astype(BF16)
        else:
            piece = acc[pl.ds(row, 384), :] * (1.0 / 1024.0)
            self.s0[...] = piece.reshape(2, 8, 24, 256).astype(BF16)


class Layer:
    groups = (("xy", "z"), ("z", "xy"))

    def __init__(self, place, refs, fins, send, recv):
        self.parts = []
        for q, (a, b) in enumerate(self.groups):
            own = tuple(refs[q * 5 : q * 5 + 5]) + (fins[q],)
            self.parts.append(Part(place, a, b, own, send.at[q], recv.at[q]))

    def begin(self, acc):
        for q, part in enumerate(self.parts):
            part.pack(acc, q * 384)
            part.step0()

    def step(self, k):
        for part in self.parts:
            getattr(part, "step%d" % k)()

    def end(self):
        for part in self.parts:
            part.drain()

    def finish_sends(self):
        for part in self.parts:
            part.finish_sends()


class BiasSum(Sender):
    groups = ("core", "xy", "z")

    def __init__(self, place, slots, send, recv):
        super().__init__(place, send, recv)
        self.slots = slots

    def begin(self, level, value):
        group, buf = self.groups[level], self.slots[level]
        i = self.p.index(group)
        buf[i] = value
        for o, to in self.p.others(group):
            self.put(buf.at[i], buf.at[i], to)

    def finish(self, level):
        self.drain()
        buf = self.slots[level]
        total = buf[0]
        for i in range(1, Place.sizes[self.groups[level]]):
            total = total + buf[i]
        return total


def kernel(
    frames,
    x_hbm, up_hbm, w1_hbm, b1, w2_hbm, b2,
    outb, ginb, fin1a, fin1b, fin2a, fin2b, biases,
    xin, xc, up, hid, s1, g2, g2h, gh, g1, pout, pin,
    w1, w2, w1t, w2t, acc1, acc2, db1, db2,
    *rest,
):
    nb = frames // R
    own = nb - 1
    bufs, rest = rest[:20], rest[20:]
    slots, rest = rest[:3], rest[3:]
    load_sem, halo_send, halo_recv, ar_send, ar_recv, bias_send, bias_recv = rest

    place = Place()
    f, r = place.f, place.r
    n = lax.axis_size("frames")
    after = (lax.rem(f + 1, n), r)
    before = (lax.rem(f + n - 1, n), r)

    barrier = pltpu.get_barrier_semaphore()
    peers = [after, before] + [to for g in Place.sizes for _, to in place.others(g)]
    for peer in peers:
        pl.semaphore_signal(barrier, inc=1, device_id=peer, device_id_type=MESH)

    tail = HX
    loads = [
        pltpu.make_async_copy(w1_hbm, w1, load_sem.at[0]),
        pltpu.make_async_copy(x_hbm.at[pl.ds(frames - tail, tail)], xin.at[pl.ds(HX + frames - tail, tail)], load_sem.at[1]),
        pltpu.make_async_copy(x_hbm.at[pl.ds(0, frames - tail)], xin.at[pl.ds(HX, frames - tail)], load_sem.at[2]),
        pltpu.make_async_copy(w2_hbm, w2, load_sem.at[3]),
        pltpu.make_async_copy(up_hbm, up, load_sem.at[4]),
        pltpu.make_async_copy(x_hbm.at[pl.ds(0, 2 * R)], xc.at[pl.ds(2 * D1, 2 * R)], load_sem.at[5]),
    ]
    for copy in loads:
        copy.start()

    def halo(k, src, dst, to):
        return pltpu.make_async_remote_copy(
            src_ref=src, dst_ref=dst, send_sem=halo_send.at[k], recv_sem=halo_recv.at[k],
            device_id=to, device_id_type=MESH,
        )

    send_x1 = halo(0, xin.at[pl.ds(HX + frames - 1024, 1024)], xin.at[pl.ds(HX - 1024, 1024)], after)
    send_x2 = halo(1, xin.at[pl.ds(HX + frames - HX, HX - 1024)], xin.at[pl.ds(0, HX - 1024)], after)
    send_p = halo(2, pout, pin, after)
    send_g2 = [halo(3 + i, g2.at[pl.ds(HH + i * D1, D1)], g2h.at[pl.ds(i * D1, D1)], before) for i in range(4)]
    send_g1 = [
        halo(7 + i, g1.at[pl.ds(HH + i * D1, D1)], g1.at[pl.ds(HH + frames + i * D1, D1)], before) for i in range(2)
    ]

    g2[pl.ds(0, HH), :] = jnp.zeros((HH, C), BF16)
    g2[pl.ds(HH + frames, HH), :] = jnp.zeros((HH, C), BF16)
    db1[...] = jnp.zeros_like(db1)
    db2[...] = jnp.zeros_like(db2)
    bias1 = b1[...].astype(F32).reshape(1, C)
    bias2 = b2[...].astype(F32).reshape(1, C)
    inner = jnp.where(f == 0, 0.0, 1.0).astype(F32)
    outer = jnp.where(f == n - 1, 0.0, 1.0).astype(F32)

    def rows(start, size=R):
        return pl.ds(start if isinstance(start, int) else pl.multiple_of(start, 256), size)

    def forward1(t, src, base, keep):
        x0 = src[rows(base + t), :]
        x1 = src[rows(base + t - D1), :]
        x2 = src[rows(base + t - 2 * D1), :]
        pre = dot(jnp.concatenate([x0, x1, x2], axis=1), w1[...]) + bias1
        act, slope = gelu_parts(pre)
        h = x0.astype(F32) + act
        hid[rows(t + HH), :] = (h if keep is None else h * keep).astype(BF16)
        s1[rows(t + HH), :] = slope

    def block_f1(b):
        forward1(b * R, xin, HX, None)

    def block_f2(b):
        t = b * R
        h = [hid[rows(t + HH - k * D2), :] for k in range(3)]
        pre = dot(jnp.concatenate(h, axis=1), w2[...]) + bias2
        act, slope = gelu_parts(pre)
        outb[rows(t), :] = (h[0].astype(F32) + act).astype(BF16)
        g = up[rows(t), :].astype(F32) * slope
        db2[...] += jnp.sum(g.reshape(R // 8, 8, C), axis=0)
        g2[rows(t + HH), :] = g.astype(BF16)

    def hidden_terms(t):
        cat = jnp.concatenate([g2[rows(t + HH + k * D2), :] for k in range(3)], axis=1)
        return dot(cat, w2t[...])

    def backward2(t, grad, summed=True):
        if not (isinstance(t, int) and t < 0):
            gh[rows(t), :] = grad
        g = grad * s1[rows(t + HH), :]
        if summed:
            db1[...] += jnp.sum(g.reshape(R // 8, 8, C), axis=0)
        g1[rows(t + HH), :] = g.astype(BF16)

    def block_b2_last():
        t = frames - R
        near, far = g2[rows(t + HH), :], g2h[...]
        mixed = jnp.concatenate([g2[rows(t + HH + D2, R - D2), :], far[:D2]], axis=0)
        terms = dot(jnp.concatenate([near, mixed, far], axis=1), w2t[...])
        backward2(t, terms + up[rows(t), :].astype(F32), False)

    def block_b2(b):
        t = b * R
        backward2(t, hidden_terms(t) + up[rows(t), :].astype(F32))

    def block_p(b):
        t = b * R
        pout[rows(t - own * R), :] = (hidden_terms(t) + up[rows(t), :].astype(F32)).astype(BF16)

    def block_b1(b):
        t = b * R
        cat = jnp.concatenate([g1[rows(t + HH + k * D1), :] for k in range(3)], axis=1)
        ginb[rows(t), :] = (dot(cat, w1t[...]) + gh[rows(t), :]).astype(BF16)

    def grad2(start, size, first=False):
        lhs = jnp.concatenate([hid[rows(start + HH - k * D2, size), :] for k in range(3)], axis=1)
        part = dot_rows(lhs, g2[rows(start + HH, size), :])
        acc2[...] = part if first else acc2[...] + part

    def grad1(start, size, first=False, src=None, base=HX):
        src = xin if src is None else src
        lhs = jnp.concatenate([src[rows(start + base - k * D1, size), :] for k in range(3)], axis=1)
        part = dot_rows(lhs, g1[rows(start + HH, size), :])
        acc1[...] = part if first else acc1[...] + part

    def loop(lo, hi, block):
        if hi - lo == 1:
            block(lo)
            return

        def body(b, _):
            block(b)
            return 0

        lax.fori_loop(lo, hi, body, 0)

    layer1 = Layer(place, bufs[:10], (fin1a, fin1b), ar_send.at[0], ar_recv.at[0])
    layer2 = Layer(place, bufs[10:], (fin2a, fin2b), ar_send.at[1], ar_recv.at[1])
    bias = BiasSum(place, slots, bias_send, bias_recv)

    loads[0].wait()
    loads[1].wait()
    block_f1(3)
    pl.semaphore_wait(barrier, len(peers))
    send_x1.start()
    send_x2.start()
    loads[2].wait()
    loop(1, 3, block_f1)
    loads[3].wait()
    loads[4].wait()
    for k in range(3):
        w2t[pl.ds(k * C, C), :] = w2[pl.ds(k * C, C), :].T
    block_f2(3)
    block_p(3)
    send_p.start()
    block_f2(2)
    block_b2(2)
    grad2(2 * R, 2 * R, True)
    grad1(2 * R, R, True)

    loads[5].wait()
    send_x1.wait_recv()
    xc[pl.ds(0, 2 * D1), :] = (xin[pl.ds(HX - 2 * D1, 2 * D1), :].astype(F32) * inner).astype(BF16)
    forward1(0, xc, 2 * D1, None)
    block_f2(1)
    send_x2.wait_recv()
    forward1(-R, xin, HX, inner)
    block_f2(0)
    send_g2[0].start()
    send_g2[1].start()
    block_b2(1)
    block_b2(0)
    send_g2[2].start()
    grad2(0, 2 * R)
    layer2.begin(acc2)
    send_g2[3].start()
    grad1(0, 2 * R, False, xc, 2 * D1)
    layer2.step(1)
    send_g1[0].start()
    send_p.wait_recv()
    backward2(-R, pin[...].astype(F32) + inner * hidden_terms(-R))
    grad1(-R, R)
    layer1.begin(acc1)
    both = jnp.concatenate(
        [jnp.sum(v[...], axis=0, keepdims=True)[:, h * 128 : (h + 1) * 128] for v in (db2, db1) for h in range(2)]
        + [jnp.zeros((4, 128), F32)],
        axis=0,
    ) * (1.0 / 1024.0)
    bias.begin(0, both)
    send_g1[1].start()
    for k in range(3):
        w1t[pl.ds(k * C, C), :] = w1[pl.ds(k * C, C), :].T
    loop(0, 2, block_b1)
    layer1.step(1)
    bias.begin(1, bias.finish(0))
    for copy in send_g2:
        copy.wait_recv()
    g2h[...] = (g2h[...].astype(F32) * outer).astype(BF16)
    block_b2_last()
    block_b1(2)
    layer2.step(2)
    for copy in send_g1:
        copy.wait_recv()
    edge = pl.ds(HH + frames, 2 * D1)
    g1[edge, :] = (g1[edge, :].astype(F32) * outer).astype(BF16)
    block_b1(3)
    layer1.step(2)
    bias.begin(2, bias.finish(1))
    layer2.step(3)
    layer1.step(3)
    biases[...] = bias.finish(2)
    layer2.step(4)
    layer1.step(4)
    layer2.end()
    for copy in [send_x1, send_x2, send_p] + send_g2 + send_g1:
        copy.wait_send()
    bias.finish_sends()
    layer2.finish_sends()
    layer1.finish_sends()
    layer1.end()


def write_kernel(outb, ginb, fin1a, fin1b, fin2a, fin2b, biases, out, gin, gw1, gb1, gw2, gb2, wide1, wide2, sem):
    copies = [pltpu.make_async_copy(outb, out, sem.at[0]), pltpu.make_async_copy(ginb, gin, sem.at[1])]
    for copy in copies:
        copy.start()
    for k, (a, b, wide, dst) in enumerate(((fin1a, fin1b, wide1, gw1), (fin2a, fin2b, wide2, gw2))):
        for h in range(2):
            wide[pl.ds(0, 384), pl.ds(h * 128, 128)] = a[:, :, h].astype(F32).reshape(384, 128)
        wide[pl.ds(384, 384), :] = b[...].astype(F32).reshape(384, 256)
        copies.append(pltpu.make_async_copy(wide, dst, sem.at[2 + k]))
        copies[-1].start()
    for h in range(2):
        gb2[:, pl.ds(h * 128, 128)] = biases[pl.ds(h, 1), :]
        gb1[:, pl.ds(h * 128, 128)] = biases[pl.ds(2 + h, 1), :]
    for copy in copies:
        copy.wait()


def body(inputs, first_layer_weight, first_layer_bias, second_layer_weight, second_layer_bias, upstream):
    _, frames, c = inputs.shape
    any_spec = pl.BlockSpec(memory_space=pl.ANY)
    vmem = pl.BlockSpec(memory_space=pltpu.VMEM)
    nb = frames // R
    scratch = [
        pltpu.VMEM((HX + frames, C), BF16),
        pltpu.VMEM((2 * R + 2 * D1, C), BF16),
        pltpu.VMEM((frames, C), BF16),
        pltpu.VMEM((HH + frames, C), BF16),
        pltpu.VMEM((HH + frames, C), F32),
        pltpu.VMEM((HH + frames + HH, C), BF16),
        pltpu.VMEM((HH, C), BF16),
        pltpu.VMEM((frames, C), F32),
        pltpu.VMEM((HH + frames + 2 * D1, C), BF16),
        pltpu.VMEM((HH, C), BF16),
        pltpu.VMEM((HH, C), BF16),
        pltpu.VMEM((3 * C, C), BF16),
        pltpu.VMEM((3 * C, C), BF16),
        pltpu.VMEM((3 * C, C), BF16),
        pltpu.VMEM((3 * C, C), BF16),
        pltpu.VMEM((3 * C, C), F32),
        pltpu.VMEM((3 * C, C), F32),
        pltpu.VMEM((8, C), F32),
        pltpu.VMEM((8, C), F32),
    ]
    scratch += [pltpu.VMEM(s, BF16) for _ in range(2) for a, b in Layer.groups for s in Part.shapes(a, b)[0]]
    fins = [Part.shapes(a, b)[1] for _ in range(2) for a, b in Layer.groups]
    scratch += [pltpu.VMEM((k, 8, 128), F32) for k in (2, 16, 8)]
    scratch += [
        pltpu.SemaphoreType.DMA((6,)),
        pltpu.SemaphoreType.DMA((9,)),
        pltpu.SemaphoreType.DMA((9,)),
        pltpu.SemaphoreType.DMA((2, 2, Part.sems)),
        pltpu.SemaphoreType.DMA((2, 2, Part.sems)),
        pltpu.SemaphoreType.DMA((23,)),
        pltpu.SemaphoreType.DMA((23,)),
    ]
    held = pl.pallas_call(
        functools.partial(kernel, frames),
        out_shape=[pltpu.VMEM((frames, c), BF16)] * 2
        + [pltpu.VMEM(shape, BF16) for shape in fins]
        + [pltpu.VMEM((8, 128), F32)],
        in_specs=[any_spec, any_spec, any_spec, vmem, any_spec, vmem],
        out_specs=[vmem] * 7,
        scratch_shapes=scratch,
        compiler_params=pltpu.CompilerParams(
            collective_id=0, has_side_effects=True, vmem_limit_bytes=58 * 1024 * 1024
        ),
    )(
        inputs.reshape(frames, c),
        upstream.reshape(frames, c),
        first_layer_weight.reshape(3 * C, C),
        first_layer_bias,
        second_layer_weight.reshape(3 * C, C),
        second_layer_bias,
    )
    outs = pl.pallas_call(
        write_kernel,
        out_shape=[
            jax.ShapeDtypeStruct((frames, c), BF16),
            jax.ShapeDtypeStruct((frames, c), BF16),
            jax.ShapeDtypeStruct((3 * C, C), F32),
            jax.ShapeDtypeStruct((1, C), F32),
            jax.ShapeDtypeStruct((3 * C, C), F32),
            jax.ShapeDtypeStruct((1, C), F32),
        ],
        in_specs=[vmem] * 7,
        out_specs=[any_spec, any_spec, any_spec, vmem, any_spec, vmem],
        scratch_shapes=[
            pltpu.VMEM((3 * C, C), F32),
            pltpu.VMEM((3 * C, C), F32),
            pltpu.SemaphoreType.DMA((4,)),
        ],
        compiler_params=pltpu.CompilerParams(vmem_limit_bytes=8 * 1024 * 1024),
    )(*held)
    out, gin, gw1, gb1, gw2, gb2 = outs
    return (
        out.reshape(1, frames, c),
        gin.reshape(1, frames, c),
        gw1.reshape(3, C, C),
        gb1.reshape(C),
        gw2.reshape(3, C, C),
        gb2.reshape(C),
    )


def solution(mesh):
    return jax.shard_map(
        body,
        mesh=mesh,
        in_specs=(P("runs", "frames", None), P(), P(), P(), P(), P("runs", "frames", None)),
        out_specs=(P("runs", "frames", None), P("runs", "frames", None), P(), P(), P(), P()),
        check_vma=False,
    )
```
